32 devices in a mesh: dom: 16 (over z, y, x), blk: 2 (over core).
Axes of the slice: x: 2, y: 2, z: 4, core: 2. Of those that a mesh axis runs over, the one named last changes fastest.
Arguments:
- pd_disp: float32 [64, 2, 128], P(('dom', 'blk')), may hold values from -4 to 4
- pd_vel: float32 [64, 2, 128], P(('dom', 'blk')), may hold values from -4 to 4
- pd_coord: float32 [64, 2, 128], P(('dom', 'blk')), may hold values from -4 to 4
- pd_modulus: float32 [64, 128], P(('dom', 'blk')), may hold values from 2 to 20
- pd_step: float32 [64, 128], P(('dom', 'blk')), may hold values from 0.03 to 0.3
- family_tile_lists: int32 [64, 3], P(('dom', 'blk')), may hold values from 0 to 11, as said below
- live_tiles: int32 [16], P('dom'), may hold values from 3 to 4, as said below
- patch_tile: int32 [32], P('dom'), may hold values from 0 to 3, as said below
- patch_blend: float32 [32, 128], P('dom'), may hold values from 0.1 to 0.9
- patch_nodes: int32 [32, 128], P(('dom', 'blk')), may hold values from 0 to 12799, as said below
- patch_matrix: float32 [32, 128, 128], P(('dom', 'blk')), may hold values from -0.5 to 0.5
- fe_disp: float32 [2, 204800], P(None, ('dom', 'blk')), may hold values from -4 to 4
- fe_vel: float32 [2, 204800], P(None, ('dom', 'blk')), may hold values from -4 to 4
- fe_step: float32 [204800], P(('dom', 'blk')), may hold values from 0.03 to 0.3
- fe_modulus: float32 [4096], P(('dom', 'blk')), may hold values from 0.5 to 2
- element_nodes: int32 [64, 4096], P(None, ('dom', 'blk')), may hold values from 0 to 12799, as said below
- shape_grad: float32 [2, 64, 64], replicated, may hold values from -0.75 to 0.75
- quad_weight: float32 [64], replicated, may hold values from 0.5 to 2
- shared_left: int32 [16, 113], P('dom'), may hold values from 0 to 12799, as said below
- shared_right: int32 [16, 113], P('dom'), may hold values from 0 to 12799, as said below
Outputs:
- pd_disp_out: float32 [64, 2, 128], P(('dom', 'blk'))
- pd_vel_out: float32 [64, 2, 128], P(('dom', 'blk'))
- fe_disp_out: float32 [2, 204800], P(None, ('dom', 'blk'))
- fe_vel_out: float32 [2, 204800], P(None, ('dom', 'blk'))
The draws below stay inside these ranges and needn't reach their ends.
Inputs may be any that keep to these rules, and one draw needn't show every extreme that they name: Local tiles at index live_tiles[d] or above in subdomain d are padding: their inputs are ignored and their outputs are zero. `family_tile_lists`: each entry names a live tile by extended index; the first subdomain names no entry below 4, the last none at 8 or above. `patch_tile`: within a subdomain the 2 patch tiles are distinct live tiles. `patch_nodes`: node ids of a subdomain's patches are distinct and belong to its elements. `element_nodes`: local node ids of each element's subdomain. `shared_left`: row d lists distinct nodes; entry r is the same physical node as shared_right[d - 1, r]. `shared_right`: row d lists distinct nodes, none in shared_left[d].
All inputs are finite; a program needn't handle non-finite values.
Results may differ from the reference program's by a relative error of at most 0.0003.
Values sent between devices are 32-bit elements; how exact they have to be, the bound alone decides.
No kernel may reach another device: no remote copies, remote signals or barrier semaphores. Data moves between devices by JAX's collectives and lax.ppermute only.
A program may use at most 64 MiB of HBM per device.

```python
import math
import jax
import jax.numpy as jnp
from jax import lax

TILE = 128
NB = 3
EX = 16
EY = 16
PT = 4
TILES = 64
PATCH_DOM = 2
PATCHES = 32
NODE_DEV = 12800
NODES = 204800
SH = 113
ELEMS = 4096
N_DOM = 16


def node_layout(key):
    base = jax.random.fold_in(key, 7)
    real_nodes = (7 * EX + 1) * (7 * EY + 1)
    keys = jax.vmap(lambda index: jax.random.fold_in(base, index))(jnp.arange(N_DOM))
    shuffle = jax.vmap(lambda sub: jax.random.permutation(sub, NODE_DEV))(keys).astype(jnp.int32)
    chosen = jax.vmap(lambda sub: jax.random.permutation(jax.random.fold_in(sub, 1), real_nodes))(keys).astype(jnp.int32)
    return (shuffle, chosen)


def tile_layout(key):
    base = jax.random.fold_in(key, 21)
    counts = jax.random.randint(jax.random.fold_in(base, 1), (N_DOM,), 3 * PT // 4, PT + 1)
    counts = counts.at[0].set(PT).at[N_DOM - 1].set(3 * PT // 4)
    return (counts.astype(jnp.int32), base)


def draw_live_tiles(key, part):
    counts, base = tile_layout(key)
    return counts


def draw_family_tile_lists(key, part):
    counts, base = tile_layout(key)
    shape = (N_DOM, PT, NB)
    side = jax.random.randint(jax.random.fold_in(base, 2), shape, 0, 3)
    domain = jnp.arange(N_DOM)[:, None, None]
    side = jnp.where((domain == 0) & (side == 0), 1, side)
    side = jnp.where((domain == N_DOM - 1) & (side == 2), 1, side)
    source = jnp.clip(domain + side - 1, 0, N_DOM - 1)
    raw = jax.random.randint(jax.random.fold_in(base, 3), shape, 0, 1 << 20)
    local = raw % counts[source]
    return (side * PT + local).reshape(TILES, NB).astype(jnp.int32)


def draw_patch_tile(key, part):
    counts, base = tile_layout(key)
    slots = jnp.arange(PT)[None, :]
    scores = jax.random.randint(jax.random.fold_in(base, 4), (N_DOM, PT), 0, 1 << 16) * PT + slots
    scores = jnp.where(slots < counts[:, None], scores, (1 << 24) + slots)
    sorting_permutation = jnp.argsort(scores, axis=1)
    return sorting_permutation[:, :PATCH_DOM].reshape(PATCHES).astype(jnp.int32)


def draw_element_nodes(key, part):
    shuffle, chosen = node_layout(key)
    rows_n = 7 * EY + 1
    element = jnp.arange(EX * EY)
    col_el = element // EY
    row_el = element % EY
    local = jnp.arange(64)
    col_n = local // 8
    row_n = local % 8
    structured = (7 * col_el[None, :] + col_n[:, None]) * rows_n + 7 * row_el[None, :] + row_n[:, None]
    mapped = jax.vmap(lambda table: table[structured])(shuffle)
    return jnp.transpose(mapped, (1, 0, 2)).reshape(64, ELEMS).astype(jnp.int32)


def draw_patch_nodes(key, part):
    shuffle, chosen = node_layout(key)
    picked = chosen[:, :PATCH_DOM * TILE]
    mapped = jax.vmap(lambda table, tile_indices: table[tile_indices])(shuffle, picked)
    return mapped.reshape(PATCHES, TILE).astype(jnp.int32)


def draw_shared_left(key, part):
    shuffle, chosen = node_layout(key)
    return shuffle[:, :SH].astype(jnp.int32)


def draw_shared_right(key, part):
    shuffle, chosen = node_layout(key)
    start = 7 * EX * (7 * EY + 1)
    return shuffle[:, start:start + SH].astype(jnp.int32)


def block_scale(key, shape, pieces, smallest, high):
    def one(position, shards_of):
        steps = jax.random.uniform(jax.random.fold_in(jax.random.fold_in(key, 6), position), (shards_of,), jnp.float32, smallest / len(pieces), high / len(pieces))
        return jnp.repeat(jnp.exp(steps), shape[position] // shards_of).reshape((-1,) + (1,) * (len(shape) - position - 1))

    factor_of = one(*pieces[0])
    for cut in pieces[1:]:
        factor_of = factor_of * one(*cut)
    return factor_of


def centred(stream_key, extent, spread, most, split=(), kind=jnp.bfloat16):
    drawn = spread * jax.random.normal(stream_key, extent, jnp.float32)
    if split:
        drawn = drawn * block_scale(stream_key, extent, split, -0.22, 0.18)
    return jnp.clip(drawn, -most, most).astype(kind)


def setup_inputs(seed: int = 0) -> dict:
    arg_keys = jax.random.split(jax.random.key(seed), 21)
    pd_disp = centred(arg_keys[0], (TILES, 2, TILE), 0.3, 4.0, ((0, 32),), jnp.float32)
    pd_vel = centred(arg_keys[1], (TILES, 2, TILE), 0.3, 4.0, ((0, 32),), jnp.float32)
    pd_coord = centred(arg_keys[2], (TILES, 2, TILE), 1.0, 4.0, ((0, 32),), jnp.float32)
    pd_modulus = jnp.clip(jnp.exp(math.log(20.0) - 2.3025851 * jax.random.uniform(arg_keys[3], (TILES, TILE), jnp.float32) ** block_scale(arg_keys[3], (TILES, TILE), ((0, 32),), -0.2, 0.2)), 2.0, 20.0)
    pd_step = jnp.clip(jnp.exp(math.log(0.3) - 2.3025852 * jax.random.uniform(arg_keys[4], (TILES, TILE), jnp.float32) ** block_scale(arg_keys[4], (TILES, TILE), ((0, 32),), -0.2, 0.2)), 0.03, 0.3)
    family_tile_lists = draw_family_tile_lists(jax.random.fold_in(arg_keys[20], 71), 0)
    live_tiles = draw_live_tiles(jax.random.fold_in(arg_keys[20], 71), 0)
    patch_tile = draw_patch_tile(jax.random.fold_in(arg_keys[20], 71), 0)
    patch_blend = jnp.clip(0.1 + 0.79999997 * jax.random.uniform(arg_keys[8], (PATCHES, TILE), jnp.float32) ** block_scale(arg_keys[8], (PATCHES, TILE), ((0, 16),), -0.2, 0.2), 0.1, 0.9)
    patch_nodes = draw_patch_nodes(jax.random.fold_in(arg_keys[20], 71), 0)
    patch_matrix = centred(arg_keys[10], (PATCHES, TILE, TILE), TILE ** -0.5, 0.5, ((0, 32),), jnp.float32)
    fe_disp = centred(arg_keys[11], (2, NODES), 0.3, 4.0, ((1, 32),), jnp.float32)
    fe_vel = centred(arg_keys[12], (2, NODES), 0.3, 4.0, ((1, 32),), jnp.float32)
    fe_step = jnp.clip(jnp.exp(math.log(0.3) - 2.3025852 * jax.random.uniform(arg_keys[13], (NODES,), jnp.float32) ** block_scale(arg_keys[13], (NODES,), ((0, 32),), -0.2, 0.2)), 0.03, 0.3)
    fe_modulus = jnp.clip(jnp.exp(math.log(2.0) - 1.3862944 * jax.random.uniform(arg_keys[14], (ELEMS,), jnp.float32) ** block_scale(arg_keys[14], (ELEMS,), ((0, 32),), -0.2, 0.2)), 0.5, 2.0)
    element_nodes = draw_element_nodes(jax.random.fold_in(arg_keys[20], 71), 0)
    shape_grad = centred(arg_keys[16], (2, 64, 64), 64 ** -0.5, 0.75, (), jnp.float32)
    quad_weight = jnp.clip(jnp.exp(jax.random.uniform(arg_keys[17], (64,), jnp.float32, math.log(0.5), math.log(2.0))), 0.5, 2.0)
    shared_left = draw_shared_left(jax.random.fold_in(arg_keys[20], 71), 0)
    shared_right = draw_shared_right(jax.random.fold_in(arg_keys[20], 71), 0)
    return {"pd_disp": pd_disp, "pd_vel": pd_vel, "pd_coord": pd_coord, "pd_modulus": pd_modulus, "pd_step": pd_step, "family_tile_lists": family_tile_lists, "live_tiles": live_tiles, "patch_tile": patch_tile, "patch_blend": patch_blend, "patch_nodes": patch_nodes, "patch_matrix": patch_matrix, "fe_disp": fe_disp, "fe_vel": fe_vel, "fe_step": fe_step, "fe_modulus": fe_modulus, "element_nodes": element_nodes, "shape_grad": shape_grad, "quad_weight": quad_weight, "shared_left": shared_left, "shared_right": shared_right}


time_step = 0.5
horizon_sq = 2.0
core_sq = 0.01
stretch_scale = 0.3
group_size = 16

def bond_terms(x_own, u_own, x_far, u_far):
    offset = x_far[:, :, None, :] - x_own[None, :, :, None]
    deformed = offset + u_far[:, :, None, :] - u_own[None, :, :, None]
    rest_sq = lax.optimization_barrier(jnp.sum(offset * offset, axis=1))
    rest_len = jnp.sqrt(rest_sq + core_sq)
    length = jnp.sqrt(lax.optimization_barrier(jnp.sum(deformed * deformed, axis=1)) + core_sq)
    stretch = length - rest_len
    ratio = stretch / stretch_scale
    influence = jnp.exp(-rest_sq / horizon_sq) / (1.0 + ratio * ratio)
    return (deformed, length, rest_len, stretch, influence)

def dilatation(x_own, u_own, x_far, u_far):
    deformed, length, rest_len, stretch, influence = bond_terms(x_own, u_own, x_far, u_far)
    point_volume = lax.optimization_barrier(jnp.sum(influence * rest_len * rest_len, axis=(0, 2)))
    volumetric_dilatation = 2.0 * lax.optimization_barrier(jnp.sum(influence * rest_len * stretch, axis=(0, 2))) / point_volume
    return (volumetric_dilatation, point_volume)

def bond_force(x_own, u_own, x_far, u_far, k_own, th_own, m_own, k_far, th_far, m_far):
    deformed, length, rest_len, stretch, influence = bond_terms(x_own, u_own, x_far, u_far)
    ko, to, mo = (k_own[None, :, None], th_own[None, :, None], m_own[None, :, None])
    kf, tf, mf = (k_far[:, None, :], th_far[:, None, :], m_far[:, None, :])
    t_own = influence * (2.0 * ko * to * rest_len / mo + 4.0 * ko * (stretch - 0.5 * to * rest_len) / mo)
    t_far = influence * (2.0 * kf * tf * rest_len / mf + 4.0 * kf * (stretch - 0.5 * tf * rest_len) / mf)
    scalar = (t_own + t_far) / length
    return lax.optimization_barrier(jnp.sum(scalar[:, None] * deformed, axis=(0, 3)))

def element_force(disp_el, modulus, shape_grad, quad_weight):
    precise = lax.Precision.HIGHEST
    grad = jnp.einsum('aqn,cne->caqe', shape_grad, disp_el, precision=precise)
    strain_xx = grad[0, 0]
    strain_yy = grad[1, 1]
    strain_xy = 0.5 * (grad[0, 1] + grad[1, 0])
    stiffen = 1.0 + strain_xx * strain_xx + strain_yy * strain_yy + 2.0 * strain_xy * strain_xy
    scaled = modulus[None, :] * quad_weight[:, None] * stiffen
    trace_sum = strain_xx + strain_yy
    s_xx = scaled * (trace_sum + 2.0 * strain_xx)
    s_yy = scaled * (trace_sum + 2.0 * strain_yy)
    s_xy = scaled * 2.0 * strain_xy
    stress = jnp.stack([jnp.stack([s_xx, s_xy]), jnp.stack([s_xy, s_yy])])
    return jnp.einsum('aqn,caqe->cne', shape_grad, stress, precision=precise)

def reference(pd_disp, pd_vel, pd_coord, pd_modulus, pd_step, family_tile_lists, live_tiles, patch_tile, patch_blend, patch_nodes, patch_matrix, fe_disp, fe_vel, fe_step, fe_modulus, element_nodes, shape_grad, quad_weight, shared_left, shared_right):
    precise = lax.Precision.HIGHEST
    tile_dom = jnp.arange(TILES, dtype=jnp.int32) // PT
    alive = (jnp.arange(TILES, dtype=jnp.int32) % PT < live_tiles[tile_dom]).astype(jnp.float32)
    far_index = family_tile_lists + (tile_dom * PT)[:, None]
    patch_dom = jnp.arange(PATCHES, dtype=jnp.int32) // PATCH_DOM
    patch_global = patch_tile + patch_dom * PT
    node_global = patch_nodes + (patch_dom * NODE_DEV)[:, None]
    elem_global = element_nodes + (jnp.arange(ELEMS, dtype=jnp.int32) // (EX * EY) * NODE_DEV)[None, :]
    dom_base = (jnp.arange(N_DOM, dtype=jnp.int32) * NODE_DEV)[:, None]
    left_global = shared_left + dom_base
    right_global = shared_right + dom_base
    coord_pad = jnp.pad(pd_coord, ((PT, PT), (0, 0), (0, 0)))
    modulus_pad = jnp.pad(pd_modulus, ((PT, PT), (0, 0)))
    tile_groups = jnp.arange(TILES, dtype=jnp.int32).reshape(-1, group_size)
    for section in range(2):
        picked = fe_disp[:, node_global]
        target = jnp.einsum('qpn,cqn->qcp', patch_matrix, picked, precision=precise)
        current = pd_disp[patch_global]
        blended = pd_disp.at[patch_global].add(patch_blend[:, None, :] * (target - current))
        disp_pad = jnp.pad(blended, ((PT, PT), (0, 0), (0, 0)))

        def dilatation_per_group(tile_indices):

            def single(tile_number):
                far = far_index[tile_number]
                return dilatation(coord_pad[PT + tile_number], disp_pad[PT + tile_number], coord_pad[far], disp_pad[far])
            return jax.vmap(single)(tile_indices)
        volumetric_dilatation, point_volume = lax.map(dilatation_per_group, tile_groups)
        volumetric_dilatation = volumetric_dilatation.reshape(TILES, TILE)
        point_volume = point_volume.reshape(TILES, TILE)
        theta_pad = jnp.pad(volumetric_dilatation, ((PT, PT), (0, 0)))
        volume_pad = jnp.pad(point_volume, ((PT, PT), (0, 0)), constant_values=1.0)

        def force_group(tile_indices):

            def single(tile_number):
                far = far_index[tile_number]
                own = PT + tile_number
                return bond_force(coord_pad[own], disp_pad[own], coord_pad[far], disp_pad[far], modulus_pad[own], theta_pad[own], volume_pad[own], modulus_pad[far], theta_pad[far], volume_pad[far])
            return jax.vmap(single)(tile_indices)
        pd_force = lax.map(force_group, tile_groups).reshape(TILES, 2, TILE)
        pd_force = pd_force * alive[:, None, None]
        pd_vel = (pd_vel + pd_step[:, None, :] * pd_force) * alive[:, None, None]
        new_disp = (blended + time_step * pd_vel) * alive[:, None, None]
        disp_el = fe_disp[:, elem_global]
        forces_el = element_force(disp_el, fe_modulus, shape_grad, quad_weight)
        nodal = jnp.zeros((2, NODES), jnp.float32).at[:, elem_global.reshape(-1)].add(forces_el.reshape(2, -1))
        nodal = -nodal
        weighted = pd_force[patch_global] * patch_blend[:, None, :]
        reaction = jnp.einsum('qpn,qcp->cqn', patch_matrix, weighted, precision=precise)
        nodal = nodal.at[:, node_global.reshape(-1)].add(reaction.reshape(2, -1))
        left_vals = nodal[:, left_global]
        right_vals = nodal[:, right_global]
        zeros_row = jnp.zeros((2, 1, SH), jnp.float32)
        from_prev = jnp.concatenate([zeros_row, right_vals[:, :-1]], axis=1)
        from_next = jnp.concatenate([left_vals[:, 1:], zeros_row], axis=1)
        nodal = nodal.at[:, left_global].add(from_prev).at[:, right_global].add(from_next)
        fe_vel = fe_vel + fe_step[None, :] * nodal
        fe_disp = fe_disp + time_step * fe_vel
        pd_disp = new_disp
    return (pd_disp, pd_vel, fe_disp, fe_vel)
```

```python
import functools

import jax
import jax.numpy as jnp
from jax import lax
from jax.experimental import pallas as pl
from jax.experimental.pallas import tpu as pltpu
from jax.sharding import PartitionSpec as P

time_step = 0.5
horizon_sq = 2.0
core_sq = 0.01
stretch_scale = 0.3

f32 = jnp.float32
bf16 = jnp.bfloat16
LANES = 128
NT = (((1,), (1,)), ((), ()))
NN = (((1,), (0,)), ((), ()))
VM = pl.BlockSpec(memory_space=pltpu.VMEM)
SM = pl.BlockSpec(memory_space=pltpu.SMEM)
HIGHEST = lax.Precision.HIGHEST


def dot(a, b, dims, precision=None):
    return lax.dot_general(a, b, dims, precision=precision, preferred_element_type=f32)


def split(x, parts):
    out = []
    for _ in range(parts):
        piece = x.astype(bf16)
        out.append(piece)
        x = x - piece.astype(f32)
    return out


class Nodes:
    def __init__(self, nodes_dev):
        self.rows_dev = nodes_dev // LANES
        self.half = -(-self.rows_dev // 8) * 8
        self.rows = 2 * self.half

    def rows_of(self, ids):
        row = ids >> 7
        return row + jnp.where(row >= self.rows_dev, self.half - self.rows_dev, 0)

    def row_mask(self, row):
        return lax.broadcasted_iota(jnp.int32, (self.rows, row.shape[1]), 0) == row

    def lane_onehot(self, ids):
        lane = ids & (LANES - 1)
        hit = lax.broadcasted_iota(jnp.int32, (LANES, ids.shape[1]), 0) == lane
        return jnp.where(hit, 1.0, 0.0).astype(bf16)

    def pick(self, table, ids, parts=3):
        pieces = jnp.concatenate(split(table, parts), axis=1)
        onehot = self.lane_onehot(ids)
        rows = dot(pieces, jnp.concatenate([onehot] * parts, axis=0), NN)
        mask = self.row_mask(self.rows_of(ids))
        n = self.rows
        return [
            jnp.sum(jnp.where(mask, rows[c * n : (c + 1) * n], 0.0), axis=0, keepdims=True)
            for c in range(2)
        ]

    def spread(self, values, ids, parts=3):
        mask = self.row_mask(self.rows_of(ids))
        placed = jnp.concatenate([jnp.where(mask, v, 0.0) for v in values], axis=0)
        onehot = self.lane_onehot(ids)
        return dot(
            jnp.concatenate(split(placed, parts), axis=1),
            jnp.concatenate([onehot] * parts, axis=1),
            NT,
        )


def blend_tiles(rank, picked, blend, patch_tile, matrices, pack):
    patches = len(matrices) // 2
    for k, matrix in enumerate(matrices):
        side, index = divmod(k, patches)
        patch = jnp.where(side == 0, rank, 1 - rank) * patches + index
        cut = slice(k * LANES, (k + 1) * LANES)
        rows = jnp.concatenate(
            [picked[0][:, cut], picked[1][:, cut], jnp.zeros((6, LANES), f32)], axis=0
        )
        target = dot(rows, matrix, NT, HIGHEST)[:2]
        tile = patch_tile[patch]
        u = pack[tile, 2:4, :]
        weight = blend[pl.ds(patch, 1), :]
        pack[tile, 2:4, :] = u + weight * (target - u)


def table_halves(nodes, rank, own, partner, table):
    r = nodes.rows_dev
    pad = jnp.zeros((nodes.half - r, LANES), f32)
    for c in range(2):
        for ref, side in ((own, rank), (partner, 1 - rank)):
            at = pl.multiple_of(c * nodes.rows + side * nodes.half, 8)
            rows = ref[pl.ds(c, r, stride=2), :]
            table[pl.ds(at, nodes.half), :] = jnp.concatenate([rows, pad], axis=0)


def start_kernel(nodes, patch_tile, f_own, f_par, s_own, s_par, ids, blend, m_own, m_par, table, pack):
    rank = lax.axis_index("blk")
    table_halves(nodes, rank, f_own, f_par, table)
    tiles = s_own.shape[0]
    for t in range(tiles):
        pack[rank * tiles + t] = s_own[t]
        pack[(1 - rank) * tiles + t] = s_par[t]
    picked = nodes.pick(table[...], ids[...])
    matrices = [m_own[p] for p in range(m_own.shape[0])] + [m_par[p] for p in range(m_par.shape[0])]
    blend_tiles(rank, picked, blend, patch_tile, matrices, pack)


def element_kernel(nodes, table, ids, modulus, quad, grad, out, cat, lanes, disp, force):
    local, elems = ids.shape
    n = nodes.rows
    block = 4
    width = block * elems
    pieces = split(table[...], 2)
    cat[:, :LANES] = pieces[0]
    cat[:, LANES:] = pieces[1]

    def block_ids(step):
        rows = [ids[pl.ds(step * block + k, 1), :] for k in range(block)]
        return jnp.concatenate(rows, axis=1)

    def gather(step, carry):
        nid = block_ids(step)
        onehot = nodes.lane_onehot(nid)
        lanes[step] = onehot
        rows = dot(cat[...], jnp.concatenate([onehot, onehot], axis=0), NN)
        mask = nodes.row_mask(nodes.rows_of(nid))
        for c in range(2):
            got = jnp.sum(jnp.where(mask, rows[c * n : (c + 1) * n], 0.0), axis=0, keepdims=True)
            for k in range(block):
                disp[pl.ds(c * local + step * block + k, 1), :] = got[:, k * elems : (k + 1) * elems]
        return carry

    lax.fori_loop(0, local // block, gather, 0)
    g = grad[...]
    half = g.shape[0] // 2
    gx = dot(g, disp[:local], NN, HIGHEST)
    gy = dot(g, disp[local:], NN, HIGHEST)
    exx = gx[:half]
    eyy = gy[half:]
    exy = 0.5 * (gx[half:] + gy[:half])
    stiffen = 1.0 + exx * exx + eyy * eyy + 2.0 * exy * exy
    scaled = modulus[...] * quad[...] * stiffen
    trace = exx + eyy
    s_xx = scaled * (trace + 2.0 * exx)
    s_yy = scaled * (trace + 2.0 * eyy)
    s_xy = scaled * 2.0 * exy
    gt = g.T
    fx = dot(gt, jnp.concatenate([s_xx, s_xy], axis=0), NN, HIGHEST)
    fy = dot(gt, jnp.concatenate([s_xy, s_yy], axis=0), NN, HIGHEST)
    both = jnp.concatenate([fx, fy], axis=0)
    high = both.astype(bf16).astype(f32)
    force[0] = high
    force[1] = both - high
    out[...] = jnp.zeros_like(out)

    def scatter(step, carry):
        nid = block_ids(step)
        mask = nodes.row_mask(nodes.rows_of(nid))
        onehot = lanes[step]
        parts = []
        for part in range(2):
            comps = []
            for c in range(2):
                rows = [
                    force[part, pl.ds(c * local + step * block + k, 1), :] for k in range(block)
                ]
                comps.append(jnp.where(mask, jnp.concatenate(rows, axis=1), 0.0))
            parts.append(jnp.concatenate(comps, axis=0).astype(bf16))
        out[...] += dot(
            jnp.concatenate(parts, axis=1), jnp.concatenate([onehot, onehot], axis=1), NT
        )
        return carry

    lax.fori_loop(0, local // block, scatter, 0)


def gather_tiles(own, left, right, ext):
    tiles = own.shape[0]
    for k, ref in enumerate((left, own, right)):
        for t in range(tiles):
            ext[k * tiles + t] = ref[t]


CHUNK = 16


def pair_terms(x0, x1, u0, u1, far):
    o0 = far[0:1] - x0
    o1 = far[1:2] - x1
    d0 = o0 + (far[2:3] - u0)
    d1 = o1 + (far[3:4] - u1)
    rest_sq = o0 * o0 + o1 * o1
    rest_len = jnp.sqrt(rest_sq + core_sq)
    length = jnp.sqrt((d0 * d0 + d1 * d1) + core_sq)
    stretch = length - rest_len
    ratio = stretch * (1.0 / stretch_scale)
    bell = jnp.exp(rest_sq * (-1.0 / horizon_sq))
    return d0, d1, rest_sq, rest_len, length, stretch, bell, 1.0 + ratio * ratio


def family(fam_own, ints_par, rank, tile, slot, tiles_dev):
    side, index = divmod(tile, tiles_dev)
    if side == 0:
        return fam_own[index, slot]
    return ints_par[index, slot]


def dilatation_kernel(fam_own, fam_par, live, own, left, right, out, ext, cols, sums):
    rank = lax.axis_index("blk")
    tiles = own.shape[0]
    dev, slots = fam_own.shape
    gather_tiles(own, left, right, ext)
    ones = jnp.ones((8, LANES), f32)
    out[...] = jnp.zeros_like(out)
    for t in range(tiles):
        side, index = divmod(t, dev)
        tile = (rank if side == 0 else 1 - rank) * dev + index
        fam = fam_own if side == 0 else fam_par

        @pl.when(tile < live[0])
        def _():
            me = ext[tiles + tile]
            turned = me.T
            for q in range(4):
                cols[q] = jnp.broadcast_to(turned[:, q : q + 1], (LANES, LANES))
            fars = [ext[fam[index, s]] for s in range(slots)]

            def chunk(i, carry):
                at = pl.multiple_of(i * CHUNK, CHUNK)
                x0, x1, u0, u1 = [cols[q, pl.ds(at, CHUNK), :] for q in range(4)]
                vol = jnp.zeros((CHUNK, LANES), f32)
                dil = jnp.zeros((CHUNK, LANES), f32)
                for far in fars:
                    _, _, rest_sq, rest_len, _, stretch, bell, soft = pair_terms(x0, x1, u0, u1, far)
                    influence = bell / soft
                    vol = vol + influence * (rest_sq + core_sq)
                    dil = dil + influence * rest_len * stretch
                sums[pl.ds(at, CHUNK), :] = vol
                sums[pl.ds(LANES + at, CHUNK), :] = dil
                return carry

            lax.fori_loop(0, LANES // CHUNK, chunk, 0)
            total = dot(ones, sums[...], NT, HIGHEST)
            volume = total[:1, :LANES]
            theta = 2.0 * total[:1, LANES:] / volume
            k = me[6:7]
            scale = 4.0 * k / volume
            out[pl.ds(tile, 1), :] = 2.0 * k * theta / volume - scale * (0.5 * theta)
            out[pl.ds(tiles + tile, 1), :] = scale


def force_kernel(
    nodes, last, fam_own, fam_par, live, patch_tile, own, left, right, ac, ac_left, ac_right,
    el_own, el_par, ids, blend, m_own, m_par, shared, *refs,
):
    if last:
        nodal, low, high, disp_out, vel_out, ext, ext2, cols, sums, held = refs
    else:
        nodal, low, high, state, ext, ext2, cols, sums, held = refs
    rank = lax.axis_index("blk")
    tiles = own.shape[0]
    dev, slots = fam_own.shape
    gather_tiles(own, left, right, ext)
    for k, ref in enumerate((ac_left, ac, ac_right)):
        for t in range(tiles):
            ext2[k * tiles + t, 0:1, :] = ref[t : t + 1, :]
            ext2[k * tiles + t, 1:2, :] = ref[tiles + t : tiles + t + 1, :]
    ones = jnp.ones((8, LANES), f32)
    held[...] = jnp.zeros_like(held)
    for t in range(tiles):
        side, index = divmod(t, dev)
        tile = (rank if side == 0 else 1 - rank) * dev + index
        fam = fam_own if side == 0 else fam_par

        @pl.when(tile < live[0])
        def _():
            me = ext[tiles + tile]
            turned = me.T
            turned2 = ext2[tiles + tile].T
            for q in range(4):
                cols[q] = jnp.broadcast_to(turned[:, q : q + 1], (LANES, LANES))
            for q in range(2):
                cols[4 + q] = jnp.broadcast_to(turned2[:, q : q + 1], (LANES, LANES))
            fars = [(ext[fam[index, s]], ext2[fam[index, s]]) for s in range(slots)]

            def chunk(i, carry):
                at = pl.multiple_of(i * CHUNK, CHUNK)
                x0, x1, u0, u1, a_own, c_own = [cols[q, pl.ds(at, CHUNK), :] for q in range(6)]
                f0 = jnp.zeros((CHUNK, LANES), f32)
                f1 = jnp.zeros((CHUNK, LANES), f32)
                for far, far2 in fars:
                    d0, d1, _, rest_len, length, stretch, bell, soft = pair_terms(x0, x1, u0, u1, far)
                    scalar = (bell / (soft * length)) * (
                        rest_len * (a_own + far2[0:1]) + stretch * (c_own + far2[1:2])
                    )
                    f0 = f0 + scalar * d0
                    f1 = f1 + scalar * d1
                sums[pl.ds(at, CHUNK), :] = f0
                sums[pl.ds(LANES + at, CHUNK), :] = f1
                return carry

            lax.fori_loop(0, LANES // CHUNK, chunk, 0)
            total = dot(ones, sums[...], NT, HIGHEST)
            force = jnp.concatenate([total[:1, :LANES], total[:1, LANES:]], axis=0)
            vel = me[4:6] + me[7:8] * force
            disp = me[2:4] + time_step * vel
            held[tile, 0:2, :] = force
            held[tile, 2:4, :] = disp
            held[tile, 4:6, :] = vel

    if last:
        for t in range(dev):
            disp_out[t] = held[rank * dev + t, 2:4, :]
            vel_out[t] = held[rank * dev + t, 4:6, :]
    else:
        for t in range(tiles):
            mine = own[t]
            now = held[t]
            state[t] = jnp.concatenate([mine[0:2], now[2:6], mine[6:8]], axis=0)
    matrices = [m_own[p] for p in range(m_own.shape[0])] + [m_par[p] for p in range(m_par.shape[0])]
    patches = m_own.shape[0]
    reactions = []
    for k, matrix in enumerate(matrices):
        side, index = divmod(k, patches)
        patch = (rank if side == 0 else 1 - rank) * patches + index
        weighted = held[patch_tile[patch], 0:2, :] * blend[pl.ds(patch, 1), :]
        rows = jnp.concatenate([weighted, jnp.zeros((6, LANES), f32)], axis=0)
        reactions.append(dot(rows, matrix, NN, HIGHEST))
    react = jnp.concatenate(reactions, axis=1)
    total = nodes.spread([react[0:1], react[1:2]], ids[...]) - (el_own[...] + el_par[...])
    nodal[...] = total
    picked = nodes.pick(total, shared[...])
    for ref, at in ((low, 0), (high, LANES)):
        ref[...] = jnp.concatenate(
            [picked[0][:, at : at + LANES], picked[1][:, at : at + LANES], jnp.zeros((6, LANES), f32)],
            axis=0,
        )


def add_border(nodes, total, shared, from_low, from_high):
    dom = lax.axis_index("dom")
    ends = lax.axis_size("dom") - 1
    low = jnp.where(dom > 0, from_low[...], 0.0)
    high = jnp.where(dom < ends, from_high[...], 0.0)
    rows = jnp.concatenate([low, high], axis=1)
    return total + nodes.spread([rows[0:1], rows[1:2]], shared)


def update_kernel(
    nodes, patch_tile, nodal, table, v_own, v_par, t_own, t_par, from_low, from_high, shared, ids,
    blend, m_own, m_par, state, table_out, vel_out, step_out, pack,
):
    rank = lax.axis_index("blk")
    r = nodes.rows_dev
    force = add_border(nodes, nodal[...], shared[...], from_low, from_high)
    table_halves(nodes, rank, v_own, v_par, vel_out)
    pad = jnp.zeros((nodes.half - r, LANES), f32)
    for ref, side in ((t_own, rank), (t_par, 1 - rank)):
        at = pl.multiple_of(side * nodes.half, 8)
        step_out[pl.ds(at, nodes.half), :] = jnp.concatenate([ref[...], pad], axis=0)
    step = step_out[...]
    vel = vel_out[...] + jnp.concatenate([step, step], axis=0) * force
    vel_out[...] = vel
    disp = table[...] + time_step * vel
    table_out[...] = disp
    pack[...] = state[...]
    picked = nodes.pick(disp, ids[...])
    matrices = [m_own[p] for p in range(m_own.shape[0])] + [m_par[p] for p in range(m_par.shape[0])]
    blend_tiles(rank, picked, blend, patch_tile, matrices, pack)


def final_kernel(nodes, nodal, table, vel, step, from_low, from_high, shared, disp_out, vel_out, f_s, v_s):
    rank = lax.axis_index("blk")
    force = add_border(nodes, nodal[...], shared[...], from_low, from_high)
    steps = step[...]
    now = vel[...] + jnp.concatenate([steps, steps], axis=0) * force
    v_s[...] = now
    f_s[...] = table[...] + time_step * now
    r = nodes.rows_dev
    for c in range(2):
        at = pl.multiple_of(c * nodes.rows + rank * nodes.half, 8)
        disp_out[pl.ds(c, r, stride=2), :] = f_s[pl.ds(at, nodes.half), :][:r]
        vel_out[pl.ds(c, r, stride=2), :] = v_s[pl.ds(at, nodes.half), :][:r]


def call(kernel, name, outs, scalars, arrays, scratch=(), flops=0):
    size = sum(a.size * 4 for a in arrays) + sum(o.size * 4 for o in outs)
    return pl.pallas_call(
        kernel,
        name=name,
        out_shape=list(outs),
        in_specs=[SM] * len(scalars) + [VM] * len(arrays),
        out_specs=[VM] * len(outs),
        scratch_shapes=list(scratch),
        cost_estimate=pl.CostEstimate(flops=flops, bytes_accessed=size, transcendentals=0),
    )(*scalars, *arrays)


def shape(*dims, dtype=f32):
    return jax.ShapeDtypeStruct(dims, dtype)


def interleaved(x):
    comps, n = x.shape
    return x.reshape(comps, n // LANES, LANES).transpose(1, 0, 2).reshape(-1, LANES)


def shards(
    pd_disp, pd_vel, pd_coord, pd_modulus, pd_step, family_tile_lists, live_tiles, patch_tile,
    patch_blend, patch_nodes, patch_matrix, fe_disp, fe_vel, fe_step, fe_modulus, element_nodes,
    shape_grad, quad_weight, shared_left, shared_right,
):
    doms = lax.axis_size("dom")
    dev = pd_disp.shape[0]
    tiles = 2 * dev
    nodes = Nodes(fe_disp.shape[1])
    n2 = 2 * nodes.rows
    local, elems = element_nodes.shape

    def swap(x):
        return lax.ppermute(x, "blk", [(0, 1), (1, 0)])

    def up(x):
        return lax.ppermute(x, "dom", [(i, (i + 1) % doms) for i in range(doms)])

    def down(x):
        return lax.ppermute(x, "dom", [((i + 1) % doms, i) for i in range(doms)])

    f_own = interleaved(fe_disp)
    v_own = interleaved(fe_vel)
    t_own = fe_step.reshape(-1, LANES)
    s_own = jnp.concatenate(
        [pd_coord, pd_disp, pd_vel, pd_modulus[:, None], pd_step[:, None]], axis=1
    )
    f_par, s_par, m_par, ids_par = swap(f_own), swap(s_own), swap(patch_matrix), swap(patch_nodes)
    fam_par = swap(family_tile_lists)
    v_par, t_par = swap(v_own), swap(t_own)
    ids = jnp.concatenate([patch_nodes, ids_par], axis=0).reshape(1, -1)
    gap = ((0, 0), (0, LANES - shared_left.shape[1]))
    shared = jnp.concatenate(
        [jnp.pad(x, gap, constant_values=-1) for x in (shared_left, shared_right)], axis=1
    )
    grad = shape_grad.reshape(-1, local)
    quad = quad_weight[:, None]
    modulus = fe_modulus[None, :]

    table, pack = call(
        functools.partial(start_kernel, nodes), "start",
        [shape(n2, LANES), shape(tiles, 8, LANES)],
        [patch_tile],
        [f_own, f_par, s_own, s_par, ids, patch_blend, patch_matrix, m_par],
    )
    for section in range(2):
        last = section == 1
        pack_left, pack_right = up(pack), down(pack)
        (el_own,) = call(
            functools.partial(element_kernel, nodes), "elements",
            [shape(n2, LANES)],
            [],
            [table, element_nodes, modulus, quad, grad],
            [
                pltpu.VMEM((n2, 2 * LANES), bf16),
                pltpu.VMEM((local // 4, LANES, 4 * elems), bf16),
                pltpu.VMEM((2 * local, elems), f32),
                pltpu.VMEM((2, 2 * local, elems), f32),
            ],
            flops=4 * 10**9,
        )
        el_par = swap(el_own)
        (ac,) = call(
            dilatation_kernel, "dilatation",
            [shape(2 * tiles, LANES)],
            [family_tile_lists, fam_par, live_tiles],
            [pack, pack_left, pack_right],
            [
                pltpu.VMEM((3 * tiles, 8, LANES), f32),
                pltpu.VMEM((4, LANES, LANES), f32),
                pltpu.VMEM((2 * LANES, LANES), f32),
            ],
        )
        ac_left, ac_right = up(ac), down(ac)
        outs = [shape(n2, LANES), shape(8, LANES), shape(8, LANES)]
        if last:
            outs += [shape(dev, 2, LANES)] * 2
        else:
            outs += [shape(tiles, 8, LANES)]
        nodal, low, high, *rest = call(
            functools.partial(force_kernel, nodes, last), "force",
            outs,
            [family_tile_lists, fam_par, live_tiles, patch_tile],
            [
                pack, pack_left, pack_right, ac, ac_left, ac_right, el_own, el_par, ids,
                patch_blend, patch_matrix, m_par, shared,
            ],
            [
                pltpu.VMEM((3 * tiles, 8, LANES), f32),
                pltpu.VMEM((3 * tiles, 8, LANES), f32),
                pltpu.VMEM((6, LANES, LANES), f32),
                pltpu.VMEM((2 * LANES, LANES), f32),
                pltpu.VMEM((tiles, 8, LANES), f32),
            ],
        )
        from_low, from_high = up(high), down(low)
        if not last:
            table, vel, step, pack = call(
                functools.partial(update_kernel, nodes), "update",
                [shape(n2, LANES), shape(n2, LANES), shape(nodes.rows, LANES), shape(tiles, 8, LANES)],
                [patch_tile],
                [
                    nodal, table, v_own, v_par, t_own, t_par, from_low, from_high, shared, ids,
                    patch_blend, patch_matrix, m_par, rest[0],
                ],
            )
        else:
            pd_disp, pd_vel = rest
            fe_disp, fe_vel = call(
                functools.partial(final_kernel, nodes), "final",
                [shape(2 * nodes.rows_dev, LANES)] * 2,
                [],
                [nodal, table, vel, step, from_low, from_high, shared],
                [pltpu.VMEM((n2, LANES), f32)] * 2,
            )

    def flat(x):
        return x.reshape(-1, 2, LANES).transpose(1, 0, 2).reshape(2, -1)

    return (pd_disp, pd_vel, flat(fe_disp), flat(fe_vel))


def solution(mesh):
    return jax.shard_map(
        shards,
        mesh=mesh,
        in_specs=(
            P(("dom", "blk"), None, None),
            P(("dom", "blk"), None, None),
            P(("dom", "blk"), None, None),
            P(("dom", "blk"), None),
            P(("dom", "blk"), None),
            P(("dom", "blk"), None),
            P("dom"),
            P("dom"),
            P("dom", None),
            P(("dom", "blk"), None),
            P(("dom", "blk"), None, None),
            P(None, ("dom", "blk")),
            P(None, ("dom", "blk")),
            P(("dom", "blk")),
            P(("dom", "blk")),
            P(None, ("dom", "blk")),
            P(),
            P(),
            P("dom", None),
            P("dom", None),
        ),
        out_specs=(
            P(("dom", "blk"), None, None),
            P(("dom", "blk"), None, None),
            P(None, ("dom", "blk")),
            P(None, ("dom", "blk")),
        ),
        check_vma=False,
    )
```

```python
import functools

import jax
import jax.numpy as jnp
from jax import lax
from jax.experimental import pallas as pl
from jax.experimental.pallas import tpu as pltpu
from jax.sharding import PartitionSpec as P


time_step = 0.5
horizon_sq = 2.0
core_sq = 0.01
stretch_scale = 0.3

f32 = jnp.float32
bf16 = jnp.bfloat16
LANES = 128
NT = (((1,), (1,)), ((), ()))
NN = (((1,), (0,)), ((), ()))
VM = pl.BlockSpec(memory_space=pltpu.VMEM)
SM = pl.BlockSpec(memory_space=pltpu.SMEM)
HBM = pl.BlockSpec(memory_space=pltpu.HBM)
HIGHEST = lax.Precision.HIGHEST


def dot(a, b, dims, precision=None):
    return lax.dot_general(a, b, dims, precision=precision, preferred_element_type=f32)


def split(x, parts):
    out = []
    for _ in range(parts):
        piece = x.astype(bf16)
        out.append(piece)
        x = x - piece.astype(f32)
    return out


class Nodes:
    def __init__(self, nodes_dev):
        self.rows_dev = nodes_dev // LANES
        self.half = -(-self.rows_dev // 8) * 8
        self.rows = 2 * self.half

    def rows_of(self, ids):
        row = ids >> 7
        return row + jnp.where(row >= self.rows_dev, self.half - self.rows_dev, 0)

    def row_mask(self, row):
        return lax.broadcasted_iota(jnp.int32, (self.rows, row.shape[1]), 0) == row

    def lane_onehot(self, ids):
        lane = ids & (LANES - 1)
        hit = lax.broadcasted_iota(jnp.int32, (LANES, ids.shape[1]), 0) == lane
        return jnp.where(hit, 1.0, 0.0).astype(bf16)

    def pick(self, table, ids, parts=3):
        pieces = jnp.concatenate(split(table, parts), axis=1)
        onehot = self.lane_onehot(ids)
        rows = dot(pieces, jnp.concatenate([onehot] * parts, axis=0), NN)
        mask = self.row_mask(self.rows_of(ids))
        n = self.rows
        return [
            jnp.sum(jnp.where(mask, rows[c * n : (c + 1) * n], 0.0), axis=0, keepdims=True)
            for c in range(2)
        ]

    def spread(self, values, ids, parts=3):
        mask = self.row_mask(self.rows_of(ids))
        placed = jnp.concatenate([jnp.where(mask, v, 0.0) for v in values], axis=0)
        onehot = self.lane_onehot(ids)
        return dot(
            jnp.concatenate(split(placed, parts), axis=1),
            jnp.concatenate([onehot] * parts, axis=1),
            NT,
        )


def blend_tiles(picked, patch_rows, matrices, pack):
    patches = matrices.shape[0]
    for k in range(patches):
        cut = slice(k * LANES, (k + 1) * LANES)
        rows = jnp.concatenate(
            [picked[0][:, cut], picked[1][:, cut], jnp.zeros((6, LANES), f32)], axis=0
        )
        target = dot(rows, matrices[k], NT, HIGHEST)[:2]
        weight = patch_rows[k : k + 1, :]
        chosen = patch_rows[patches + k : patches + k + 1, :]
        for t in range(pack.shape[0]):
            u = pack[t, 2:4, :]
            pack[t, 2:4, :] = u + jnp.where(chosen == float(t), weight * (target - u), 0.0)


class Parcel:
    def __init__(self, nodes, tiles, patches, local):
        self.tiles, self.patches = tiles, patches
        sizes = [
            ("disp", 2 * nodes.half), ("vel", 2 * nodes.half), ("step", nodes.half),
            ("points", 8 * tiles), ("matrix", LANES * patches),
            ("misc", 8 * -(-(7 * patches + 4) // 8)), ("elements", local), ("grad", 2 * local),
        ]
        self.at, row = {}, 0
        for name, size in sizes:
            self.at[name] = slice(row, row + size)
            row += size
        self.rows = row
        first = self.at["misc"].start
        counts = [
            ("nodes", patches), ("quad", 1), ("modulus", 1), ("blend", 2 * patches), ("left", 1),
            ("right", 1), ("tile", 2 * patches),
        ]
        for name, size in counts:
            self.at[name] = slice(first, first + size)
            first += size


def pack_kernel(nodes, parcel, count, *refs):
    given, out, held, sem = refs[:count], refs[count], refs[count + 1 : -1], refs[-1]
    copies = [pltpu.make_async_copy(a, b, sem.at[k]) for k, (a, b) in enumerate(zip(given, held))]
    for copy in copies:
        copy.start()
    for copy in copies:
        copy.wait()
    (
        matrix, ids, disp, x, u, v, k, step, vel, mass_step, left, right, elements, grad, quad,
        modulus, blend, patch_tile,
    ) = held
    pad = jnp.zeros((nodes.half - nodes.rows_dev, LANES), f32)
    for name, flat in (("disp", disp), ("vel", vel)):
        rows = []
        for c in range(2):
            rows += [flat[c : c + 1, i * LANES : (i + 1) * LANES] for i in range(nodes.rows_dev)]
            rows.append(pad)
        out[parcel.at[name], :] = jnp.concatenate(rows, axis=0)
    out[parcel.at["step"], :] = jnp.concatenate([mass_step[...], pad], axis=0)
    rows = []
    for t in range(parcel.tiles):
        rows += [x[t], u[t], v[t], k[t : t + 1, :], step[t : t + 1, :]]
    out[parcel.at["points"], :] = jnp.concatenate(rows, axis=0)
    for p in range(parcel.patches):
        first = parcel.at["matrix"].start + p * LANES
        out[first : first + LANES, :] = matrix[p]
    out[parcel.at["misc"], :] = jnp.full((parcel.at["misc"].stop - parcel.at["misc"].start, LANES), -1.0, f32)
    for name, ref in (
        ("nodes", ids), ("quad", quad), ("modulus", modulus), ("blend", blend), ("left", left), ("right", right),
    ):
        out[parcel.at[name], : ref.shape[1]] = ref[...].astype(f32)
    for p in range(2 * parcel.patches):
        row = parcel.at["tile"].start + p
        out[row : row + 1, :] = jnp.full((1, LANES), patch_tile[p], jnp.int32).astype(f32)
    out[parcel.at["elements"], :] = elements[...].astype(f32)
    out[parcel.at["grad"], : grad.shape[1]] = grad[...]


def start_kernel(
    nodes, parcel, own, partner, table, vel, step, pack, matrices, ids, shared, patch_rows, elements,
    grad, quad, modulus,
):
    rank = lax.axis_index("blk")
    half, tiles, patches = nodes.half, parcel.tiles, parcel.patches
    for order, (side, ref) in enumerate(((rank, own), (1 - rank, partner))):
        for name, out in (("disp", table), ("vel", vel)):
            for c in range(2):
                at = pl.multiple_of(c * nodes.rows + side * half, 8)
                first = parcel.at[name].start + c * half
                out[pl.ds(at, half), :] = ref[first : first + half, :]
        step[pl.ds(pl.multiple_of(side * half, 8), half), :] = ref[parcel.at["step"], :]
        for t in range(tiles):
            first = parcel.at["points"].start + 8 * t
            pack[side * tiles + t] = ref[first : first + 8, :]
        for p in range(patches):
            k = order * patches + p
            first = parcel.at["matrix"].start + p * LANES
            matrices[k] = ref[first : first + LANES, :]
            row = parcel.at["nodes"].start + p
            ids[:, k * LANES : (k + 1) * LANES] = ref[row : row + 1, :].astype(jnp.int32)
            for n, name in enumerate(("blend", "tile")):
                row = parcel.at[name].start + side * patches + p
                patch_rows[2 * patches * n + k : 2 * patches * n + k + 1, :] = own[pl.ds(row, 1), :]
    for n, name in enumerate(("left", "right")):
        shared[:, n * LANES : (n + 1) * LANES] = own[parcel.at[name], :].astype(jnp.int32)
    elements[...] = own[parcel.at["elements"], :].astype(jnp.int32)
    grad[...] = own[parcel.at["grad"], : grad.shape[1]]
    quad[...] = own[parcel.at["quad"], : quad.shape[1]]
    modulus[...] = own[parcel.at["modulus"], :]
    picked = nodes.pick(table[...], ids[...])
    blend_tiles(picked, patch_rows, matrices, pack)


BLOCK = 4


def block_ids(ids, step):
    return jnp.concatenate([ids[pl.ds(step * BLOCK + k, 1), :] for k in range(BLOCK)], axis=1)


def stress_kernel(nodes, table, ids, modulus, quad, grad, force, cat, disp):
    local, elems = ids.shape
    n = nodes.rows
    pieces = split(table[...], 2)
    cat[:, :LANES] = pieces[0]
    cat[:, LANES:] = pieces[1]

    def gather(step, carry):
        nid = block_ids(ids, step)
        onehot = nodes.lane_onehot(nid)
        rows = dot(cat[...], jnp.concatenate([onehot, onehot], axis=0), NN)
        mask = nodes.row_mask(nodes.rows_of(nid))
        for c in range(2):
            got = jnp.sum(jnp.where(mask, rows[c * n : (c + 1) * n], 0.0), axis=0, keepdims=True)
            for k in range(BLOCK):
                disp[pl.ds(c * local + step * BLOCK + k, 1), :] = got[:, k * elems : (k + 1) * elems]
        return carry

    lax.fori_loop(0, local // BLOCK, gather, 0)
    g = grad[...]
    half = g.shape[0] // 2
    gx = dot(g, disp[:local], NN, HIGHEST)
    gy = dot(g, disp[local:], NN, HIGHEST)
    exx = gx[:half]
    eyy = gy[half:]
    exy = 0.5 * (gx[half:] + gy[:half])
    stiffen = 1.0 + exx * exx + eyy * eyy + 2.0 * exy * exy
    weights = jnp.broadcast_to(quad[...], (half, half))
    eye = lax.broadcasted_iota(jnp.int32, (half, half), 0) == lax.broadcasted_iota(
        jnp.int32, (half, half), 1
    )
    column = jnp.sum(jnp.where(eye, weights, 0.0), axis=1, keepdims=True)
    scaled = modulus[...] * column * stiffen
    trace = exx + eyy
    s_xx = scaled * (trace + 2.0 * exx)
    s_yy = scaled * (trace + 2.0 * eyy)
    s_xy = scaled * 2.0 * exy
    gt = g.T
    fx = dot(gt, jnp.concatenate([s_xx, s_xy], axis=0), NN, HIGHEST)
    fy = dot(gt, jnp.concatenate([s_xy, s_yy], axis=0), NN, HIGHEST)
    both = jnp.concatenate([fx, fy], axis=0)
    high = both.astype(bf16).astype(f32)
    force[0] = high
    force[1] = both - high


def assembly_kernel(nodes, ids, force, out):
    local, _ = ids.shape
    out[...] = jnp.zeros_like(out)

    def scatter(step, carry):
        nid = block_ids(ids, step)
        mask = nodes.row_mask(nodes.rows_of(nid))
        onehot = nodes.lane_onehot(nid)
        parts = []
        for part in range(2):
            comps = []
            for c in range(2):
                rows = [
                    force[part, pl.ds(c * local + step * BLOCK + k, 1), :] for k in range(BLOCK)
                ]
                comps.append(jnp.where(mask, jnp.concatenate(rows, axis=1), 0.0))
            parts.append(jnp.concatenate(comps, axis=0).astype(bf16))
        out[...] += dot(
            jnp.concatenate(parts, axis=1), jnp.concatenate([onehot, onehot], axis=1), NT
        )
        return carry

    lax.fori_loop(0, local // BLOCK, scatter, 0)


def gather_tiles(own, left, right, ext):
    tiles = own.shape[0]
    for k, ref in enumerate((left, own, right)):
        for t in range(tiles):
            tile = ref[t]
            ext[k * tiles + t] = jnp.concatenate(
                [tile[0:2], tile[0:2] + tile[2:4], tile[4:8]], axis=0
            )


CHUNK = 16


def pair_terms(x0, x1, y0, y1, far):
    o0 = far[0:1] - x0
    o1 = far[1:2] - x1
    d0 = far[2:3] - y0
    d1 = far[3:4] - y1
    rest_sq = o0 * o0 + o1 * o1
    rest_core = rest_sq + core_sq
    rest_len = rest_core * lax.rsqrt(rest_core)
    length_sq = (d0 * d0 + d1 * d1) + core_sq
    length = length_sq * lax.rsqrt(length_sq)
    stretch = length - rest_len
    bell = jnp.exp(rest_sq * (-1.0 / horizon_sq))
    soft = 1.0 + stretch * stretch * (1.0 / stretch_scale**2)
    return d0, d1, rest_core, rest_len, length, stretch, bell, soft


def dilatation_kernel(fam_own, fam_par, live, own, left, right, out, ext, cols, sums):
    rank = lax.axis_index("blk")
    tiles = own.shape[0]
    dev, slots = fam_own.shape
    gather_tiles(own, left, right, ext)
    ones = jnp.ones((8, LANES), f32)
    out[...] = jnp.zeros_like(out)
    for t in range(tiles):
        side, index = divmod(t, dev)
        tile = (rank if side == 0 else 1 - rank) * dev + index
        fam = fam_own if side == 0 else fam_par

        @pl.when(tile < live[0])
        def _():
            me = ext[tiles + tile]
            turned = me.T
            for q in range(4):
                cols[q] = jnp.broadcast_to(turned[:, q : q + 1], (LANES, LANES))
            fars = [ext[fam[index, s]] for s in range(slots)]

            def chunk(i, carry):
                at = pl.multiple_of(i * CHUNK, CHUNK)
                x0, x1, u0, u1 = [cols[q, pl.ds(at, CHUNK), :] for q in range(4)]
                vol = jnp.zeros((CHUNK, LANES), f32)
                dil = jnp.zeros((CHUNK, LANES), f32)
                for far in fars:
                    _, _, rest_core, rest_len, _, stretch, bell, soft = pair_terms(x0, x1, u0, u1, far)
                    influence = bell * pl.reciprocal(soft)
                    vol = vol + influence * rest_core
                    dil = dil + influence * rest_len * stretch
                sums[pl.ds(at, CHUNK), :] = vol
                sums[pl.ds(LANES + at, CHUNK), :] = dil
                return carry

            lax.fori_loop(0, LANES // CHUNK, chunk, 0)
            total = dot(ones, sums[...], NT, HIGHEST)
            volume = total[:1, :LANES]
            theta = 2.0 * total[:1, LANES:] / volume
            k = me[6:7]
            scale = 4.0 * k / volume
            out[pl.ds(tile, 1), :] = 2.0 * k * theta / volume - scale * (0.5 * theta)
            out[pl.ds(tiles + tile, 1), :] = scale


def bond_kernel(fam_own, fam_par, live, own, left, right, bonds, own_sums, ext, cols, sums):
    rank = lax.axis_index("blk")
    tiles = own.shape[0]
    dev, slots = fam_own.shape
    gather_tiles(own, left, right, ext)
    ones = jnp.ones((8, LANES), f32)
    for t in range(tiles):
        side, index = divmod(t, dev)
        tile = (rank if side == 0 else 1 - rank) * dev + index
        fam = fam_own if side == 0 else fam_par

        @pl.when(tile < live[0])
        def _():
            turned = ext[tiles + tile].T
            for q in range(4):
                cols[q] = jnp.broadcast_to(turned[:, q : q + 1], (LANES, LANES))
            fars = [ext[fam[index, s]] for s in range(slots)]

            def chunk(i, carry):
                at = pl.multiple_of(i * CHUNK, CHUNK)
                x0, x1, u0, u1 = [cols[q, pl.ds(at, CHUNK), :] for q in range(4)]
                acc = [jnp.zeros((CHUNK, LANES), f32)] * 4
                for s, far in enumerate(fars):
                    d0, d1, _, rest_len, length, stretch, bell, soft = pair_terms(x0, x1, u0, u1, far)
                    over = bell * pl.reciprocal(soft * length)
                    by_rest = over * rest_len
                    by_stretch = over * stretch
                    terms = [by_rest * d0, by_rest * d1, by_stretch * d0, by_stretch * d1]
                    for q, term in enumerate(terms):
                        bonds[tile, s, q, pl.ds(at, CHUNK), :] = term
                    acc = [a + term for a, term in zip(acc, terms)]
                for q in range(4):
                    sums[pl.ds(q * LANES + at, CHUNK), :] = acc[q]
                return carry

            lax.fori_loop(0, LANES // CHUNK, chunk, 0)
            total = dot(ones, sums[...], NT, HIGHEST)
            for q in range(4):
                own_sums[tile, q : q + 1, :] = total[:1, q * LANES : (q + 1) * LANES]


def force_kernel(
    nodes, last, fam_own, fam_par, live, pack, ac, ac_left, ac_right, bonds, own_sums,
    el_own, el_par, ids, matrices, patch_rows, shared, *refs,
):
    if last:
        nodal, low, high, disp_out, vel_out, ext, sums, held = refs
    else:
        nodal, low, high, state, ext, sums, held = refs
    rank = lax.axis_index("blk")
    tiles = pack.shape[0]
    dev, slots = fam_own.shape
    for k, ref in enumerate((ac_left, ac, ac_right)):
        for t in range(tiles):
            ext[k * tiles + t, 0:1, :] = ref[t : t + 1, :]
            ext[k * tiles + t, 1:2, :] = ref[tiles + t : tiles + t + 1, :]
    ones = jnp.ones((8, LANES), f32)
    held[...] = jnp.zeros_like(held)
    for t in range(tiles):
        side, index = divmod(t, dev)
        tile = (rank if side == 0 else 1 - rank) * dev + index
        fam = fam_own if side == 0 else fam_par

        @pl.when(tile < live[0])
        def _():
            me = pack[tile]
            mine = ext[tiles + tile]
            fars = [ext[fam[index, s]] for s in range(slots)]

            def chunk(i, carry):
                at = pl.multiple_of(i * CHUNK, CHUNK)
                f = [jnp.zeros((CHUNK, LANES), f32)] * 2
                for s, far in enumerate(fars):
                    w = [bonds[tile, s, q, pl.ds(at, CHUNK), :] for q in range(4)]
                    f = [f[c] + (w[c] * far[0:1] + w[2 + c] * far[1:2]) for c in range(2)]
                for c in range(2):
                    sums[pl.ds(c * LANES + at, CHUNK), :] = f[c]
                return carry

            lax.fori_loop(0, LANES // CHUNK, chunk, 0)
            total = dot(ones, sums[...], NT, HIGHEST)
            far_part = jnp.concatenate([total[:1, :LANES], total[:1, LANES:]], axis=0)
            near = own_sums[tile]
            force = (near[0:2] * mine[0:1] + near[2:4] * mine[1:2]) + far_part
            vel = me[4:6] + me[7:8] * force
            disp = me[2:4] + time_step * vel
            held[tile, 0:2, :] = force
            held[tile, 2:4, :] = disp
            held[tile, 4:6, :] = vel

    if last:
        for t in range(dev):
            disp_out[t] = held[rank * dev + t, 2:4, :]
            vel_out[t] = held[rank * dev + t, 4:6, :]
    else:
        for t in range(tiles):
            mine = pack[t]
            now = held[t]
            state[t] = jnp.concatenate([mine[0:2], now[2:6], mine[6:8]], axis=0)
    patches = matrices.shape[0]
    reactions = []
    for k in range(patches):
        chosen = patch_rows[patches + k : patches + k + 1, :]
        force = jnp.zeros((2, LANES), f32)
        for t in range(tiles):
            force = force + jnp.where(chosen == float(t), held[t, 0:2, :], 0.0)
        weighted = force * patch_rows[k : k + 1, :]
        rows = jnp.concatenate([weighted, jnp.zeros((6, LANES), f32)], axis=0)
        reactions.append(dot(rows, matrices[k], NN, HIGHEST))
    react = jnp.concatenate(reactions, axis=1)
    total = nodes.spread([react[0:1], react[1:2]], ids[...]) - (el_own[...] + el_par[...])
    nodal[...] = total
    picked = nodes.pick(total, shared[...])
    for ref, at in ((low, 0), (high, LANES)):
        ref[...] = jnp.concatenate(
            [picked[0][:, at : at + LANES], picked[1][:, at : at + LANES], jnp.zeros((6, LANES), f32)],
            axis=0,
        )


def add_border(nodes, total, shared, from_low, from_high):
    dom = lax.axis_index("dom")
    ends = lax.axis_size("dom") - 1
    low = jnp.where(dom > 0, from_low[...], 0.0)
    high = jnp.where(dom < ends, from_high[...], 0.0)
    rows = jnp.concatenate([low, high], axis=1)
    return total + nodes.spread([rows[0:1], rows[1:2]], shared)


def update_kernel(
    nodes, nodal, table, vel, step, from_low, from_high, shared, ids, matrices, patch_rows, state,
    table_out, vel_out, pack,
):
    force = add_border(nodes, nodal[...], shared[...], from_low, from_high)
    steps = step[...]
    now = vel[...] + jnp.concatenate([steps, steps], axis=0) * force
    vel_out[...] = now
    disp = table[...] + time_step * now
    table_out[...] = disp
    pack[...] = state[...]
    picked = nodes.pick(disp, ids[...])
    blend_tiles(picked, patch_rows, matrices, pack)


def final_kernel(
    nodes, nodal, table, vel, step, from_low, from_high, shared, disp_out, vel_out, f_s, v_s,
):
    rank = lax.axis_index("blk")
    force = add_border(nodes, nodal[...], shared[...], from_low, from_high)
    steps = step[...]
    now = vel[...] + jnp.concatenate([steps, steps], axis=0) * force
    v_s[...] = now
    f_s[...] = table[...] + time_step * now
    for out, held in ((disp_out, f_s), (vel_out, v_s)):
        for c in range(2):
            at = pl.multiple_of(c * nodes.rows + rank * nodes.half, 8)
            rows = held[pl.ds(at, nodes.half), :]
            for i in range(nodes.rows_dev):
                out[c : c + 1, i * LANES : (i + 1) * LANES] = rows[i : i + 1]


def call(kernel, outs, scalars, arrays, scratch=(), flops=0, vmem=4, spec=VM):
    size = sum(a.size * 4 for a in arrays) + sum(o.size * 4 for o in outs)
    return pl.pallas_call(
        kernel,
        out_shape=list(outs),
        in_specs=[SM] * len(scalars) + [spec] * len(arrays),
        out_specs=[VM] * len(outs),
        scratch_shapes=list(scratch),
        cost_estimate=pl.CostEstimate(flops=flops, bytes_accessed=size, transcendentals=0),
        compiler_params=pltpu.CompilerParams(vmem_limit_bytes=int(vmem * 2**20)),
    )(*scalars, *arrays)


def shape(*dims, dtype=f32):
    return jax.ShapeDtypeStruct(dims, dtype)


def shards(
    pd_disp, pd_vel, pd_coord, pd_modulus, pd_step, family_tile_lists, live_tiles, patch_tile,
    patch_blend, patch_nodes, patch_matrix, fe_disp, fe_vel, fe_step, fe_modulus, element_nodes,
    shape_grad, quad_weight, shared_left, shared_right,
):
    doms = lax.axis_size("dom")
    dev = pd_disp.shape[0]
    tiles = 2 * dev
    patches = patch_matrix.shape[0]
    slots = family_tile_lists.shape[1]
    nodes = Nodes(fe_disp.shape[1])
    n2 = 2 * nodes.rows
    local, elems = element_nodes.shape

    def swap(x):
        return lax.ppermute(x, "blk", [(0, 1), (1, 0)])

    def up(x):
        return lax.ppermute(x, "dom", [(i, (i + 1) % doms) for i in range(doms)])

    def down(x):
        return lax.ppermute(x, "dom", [((i + 1) % doms, i) for i in range(doms)])

    given = [
        patch_matrix, patch_nodes, fe_disp, pd_coord, pd_disp, pd_vel, pd_modulus, pd_step, fe_vel,
        fe_step.reshape(-1, LANES), shared_left, shared_right, element_nodes,
        shape_grad.reshape(-1, local), quad_weight[None, :], fe_modulus[None, :], patch_blend,
        patch_tile,
    ]
    spaces = [pltpu.VMEM] * (len(given) - 1) + [pltpu.SMEM]
    parcel = Parcel(nodes, dev, patches, local)
    (own,) = call(
        functools.partial(pack_kernel, nodes, parcel, len(given)),
        [shape(parcel.rows, LANES)],
        [], given,
        [space(x.shape, x.dtype) for space, x in zip(spaces, given)]
        + [pltpu.SemaphoreType.DMA((len(given),))],
        spec=HBM,
        vmem=63,
    )
    partner = swap(own)
    fam_par = swap(family_tile_lists)
    lists = [family_tile_lists, fam_par, live_tiles]
    int32 = jnp.int32
    table, vel, step, pack, matrices, ids, shared, patch_rows, elements, grad, quad, modulus = call(
        functools.partial(start_kernel, nodes, parcel),
        [
            shape(n2, LANES), shape(n2, LANES), shape(nodes.rows, LANES), shape(tiles, 8, LANES),
            shape(2 * patches, LANES, LANES), shape(1, 2 * patches * LANES, dtype=int32),
            shape(1, 2 * LANES, dtype=int32), shape(4 * patches, LANES),
            shape(local, elems, dtype=int32), shape(2 * local, local), shape(1, local), shape(1, elems),
        ],
        [],
        [own, partner],
    )
    for section in range(2):
        last = section == 1
        packs = [pack, up(pack), down(pack)]
        (force_el,) = call(
            functools.partial(stress_kernel, nodes),
            [shape(2, 2 * local, elems)],
            [],
            [table, elements, modulus, quad, grad],
            [pltpu.VMEM((n2, 2 * LANES), bf16), pltpu.VMEM((2 * local, elems), f32)],
            flops=10**9, vmem=8,
        )
        (ac,) = call(
            dilatation_kernel,
            [shape(2 * tiles, LANES)],
            lists,
            packs,
            [
                pltpu.VMEM((3 * tiles, 8, LANES), f32),
                pltpu.VMEM((4, LANES, LANES), f32),
                pltpu.VMEM((2 * LANES, LANES), f32),
            ],
        )
        acs = [ac, up(ac), down(ac)]
        (el_own,) = call(
            functools.partial(assembly_kernel, nodes),
            [shape(n2, LANES)],
            [],
            [elements, force_el],
            flops=10**9, vmem=8,
        )
        el_par = swap(el_own)
        bonds, own_sums = call(
            bond_kernel,
            [shape(tiles, slots, 4, LANES, LANES), shape(tiles, 8, LANES)],
            lists,
            packs,
            [
                pltpu.VMEM((3 * tiles, 8, LANES), f32),
                pltpu.VMEM((4, LANES, LANES), f32),
                pltpu.VMEM((4 * LANES, LANES), f32),
            ],
            vmem=8,
        )
        outs = [shape(n2, LANES), shape(8, LANES), shape(8, LANES)]
        if last:
            outs += [shape(dev, 2, LANES)] * 2
        else:
            outs += [shape(tiles, 8, LANES)]
        nodal, low, high, *rest = call(
            functools.partial(force_kernel, nodes, last),
            outs,
            lists,
            [
                pack, *acs, bonds, own_sums, el_own, el_par, ids, matrices, patch_rows,
                shared,
            ],
            [
                pltpu.VMEM((3 * tiles, 8, LANES), f32),
                pltpu.VMEM((2 * LANES, LANES), f32),
                pltpu.VMEM((tiles, 8, LANES), f32),
            ],
            vmem=8,
        )
        from_low, from_high = up(high), down(low)
        if not last:
            table, vel, pack = call(
                functools.partial(update_kernel, nodes),
                [shape(n2, LANES), shape(n2, LANES), shape(tiles, 8, LANES)],
                [],
                [
                    nodal, table, vel, step, from_low, from_high, shared, ids, matrices,
                    patch_rows, rest[0],
                ],
            )
        else:
            pd_disp, pd_vel = rest
            fe_disp, fe_vel = call(
                functools.partial(final_kernel, nodes),
                [shape(*fe_disp.shape)] * 2,
                [],
                [nodal, table, vel, step, from_low, from_high, shared],
                [pltpu.VMEM((n2, LANES), f32)] * 2,
            )
    return (pd_disp, pd_vel, fe_disp, fe_vel)


def solution(mesh):
    return jax.shard_map(
        shards,
        mesh=mesh,
        in_specs=(
            P(("dom", "blk"), None, None),
            P(("dom", "blk"), None, None),
            P(("dom", "blk"), None, None),
            P(("dom", "blk"), None),
            P(("dom", "blk"), None),
            P(("dom", "blk"), None),
            P("dom"),
            P("dom"),
            P("dom", None),
            P(("dom", "blk"), None),
            P(("dom", "blk"), None, None),
            P(None, ("dom", "blk")),
            P(None, ("dom", "blk")),
            P(("dom", "blk")),
            P(("dom", "blk")),
            P(None, ("dom", "blk")),
            P(),
            P(),
            P("dom", None),
            P("dom", None),
        ),
        out_specs=(
            P(("dom", "blk"), None, None),
            P(("dom", "blk"), None, None),
            P(None, ("dom", "blk")),
            P(None, ("dom", "blk")),
        ),
        check_vma=False,
    )
```

```python
import functools

import jax
import jax.numpy as jnp
from jax import lax
from jax.experimental import pallas as pl
from jax.experimental.pallas import tpu as pltpu
from jax.sharding import PartitionSpec as P


time_step = 0.5
horizon_sq = 2.0
core_sq = 0.01
stretch_scale = 0.3

f32 = jnp.float32
bf16 = jnp.bfloat16
LANES = 128
NT = (((1,), (1,)), ((), ()))
NN = (((1,), (0,)), ((), ()))
VM = pl.BlockSpec(memory_space=pltpu.VMEM)
SM = pl.BlockSpec(memory_space=pltpu.SMEM)
HBM = pl.BlockSpec(memory_space=pltpu.HBM)
HIGHEST = lax.Precision.HIGHEST


def dot(a, b, dims, precision=None):
    return lax.dot_general(a, b, dims, precision=precision, preferred_element_type=f32)


def split(x, parts):
    out = []
    for _ in range(parts):
        piece = x.astype(bf16)
        out.append(piece)
        x = x - piece.astype(f32)
    return out


class Nodes:
    def __init__(self, nodes_dev):
        self.rows_dev = nodes_dev // LANES
        self.half = -(-self.rows_dev // 8) * 8
        self.rows = 2 * self.half

    def rows_of(self, ids):
        row = ids >> 7
        return row + jnp.where(row >= self.rows_dev, self.half - self.rows_dev, 0)

    def row_mask(self, row):
        return lax.broadcasted_iota(jnp.int32, (self.rows, row.shape[1]), 0) == row

    def lane_onehot(self, ids):
        lane = ids & (LANES - 1)
        hit = lax.broadcasted_iota(jnp.int32, (LANES, ids.shape[1]), 0) == lane
        return jnp.where(hit, 1.0, 0.0).astype(bf16)

    def wide_rows(self, table):
        half = [table[pl.ds(k, self.rows, stride=2), :] for k in range(2)]
        return jnp.concatenate(half, axis=1)

    def wide_masks(self, ids):
        row = self.rows_of(ids)
        lane = ((row & 1) << 7) | (ids & (LANES - 1))
        count = ids.shape[1]
        mask = lax.broadcasted_iota(jnp.int32, (self.rows // 2, count), 0) == row >> 1
        hit = lax.broadcasted_iota(jnp.int32, (2 * LANES, count), 0) == lane
        return mask, jnp.where(hit, 1.0, 0.0).astype(bf16)

    def pick(self, table, ids, parts=3):
        pieces = jnp.concatenate(split(table, parts), axis=1)
        onehot = self.lane_onehot(ids)
        rows = dot(pieces, jnp.concatenate([onehot] * parts, axis=0), NN)
        mask = self.row_mask(self.rows_of(ids))
        n = self.rows
        return [
            jnp.sum(jnp.where(mask, rows[c * n : (c + 1) * n], 0.0), axis=0, keepdims=True)
            for c in range(2)
        ]

    def spread(self, values, ids, parts=3):
        mask = self.row_mask(self.rows_of(ids))
        placed = jnp.concatenate([jnp.where(mask, v, 0.0) for v in values], axis=0)
        onehot = self.lane_onehot(ids)
        return dot(
            jnp.concatenate(split(placed, parts), axis=1),
            jnp.concatenate([onehot] * parts, axis=1),
            NT,
        )


def blend_tiles(picked, patch_rows, matrices, pack):
    patches = matrices.shape[0]
    for k in range(patches):
        cut = slice(k * LANES, (k + 1) * LANES)
        rows = jnp.concatenate(
            [picked[0][:, cut], picked[1][:, cut], jnp.zeros((6, LANES), f32)], axis=0
        )
        target = dot(rows, matrices[k], NT, HIGHEST)[:2]
        weight = patch_rows[k : k + 1, :]
        chosen = patch_rows[patches + k : patches + k + 1, :]
        for t in range(pack.shape[0]):
            u = pack[t, 2:4, :]
            pack[t, 2:4, :] = u + jnp.where(chosen == float(t), weight * (target - u), 0.0)


class Parcel:
    def __init__(self, nodes, tiles, patches, local):
        self.tiles, self.patches = tiles, patches
        sizes = [
            ("disp", 2 * nodes.half), ("vel", 2 * nodes.half), ("step", nodes.half),
            ("points", 8 * tiles), ("matrix", LANES * patches),
            ("misc", 8 * -(-(7 * patches + 4) // 8)), ("elements", local), ("grad", 2 * local),
        ]
        self.at, row = {}, 0
        for name, size in sizes:
            self.at[name] = slice(row, row + size)
            row += size
        self.rows = row
        first = self.at["misc"].start
        counts = [
            ("nodes", patches), ("quad", 1), ("modulus", 1), ("blend", 2 * patches), ("left", 1),
            ("right", 1), ("tile", 2 * patches),
        ]
        for name, size in counts:
            self.at[name] = slice(first, first + size)
            first += size


def pack_kernel(nodes, parcel, count, *refs):
    given, out, held, sem = refs[:count], refs[count], refs[count + 1 : -1], refs[-1]
    copies = [pltpu.make_async_copy(a, b, sem.at[k]) for k, (a, b) in enumerate(zip(given, held))]
    for copy in copies:
        copy.start()
    for copy in copies:
        copy.wait()
    (
        matrix, ids, disp, x, u, v, k, step, vel, mass_step, left, right, elements, grad, quad,
        modulus, blend, patch_tile,
    ) = held
    pad = jnp.zeros((nodes.half - nodes.rows_dev, LANES), f32)
    for name, flat in (("disp", disp), ("vel", vel)):
        rows = []
        for c in range(2):
            rows += [flat[c : c + 1, i * LANES : (i + 1) * LANES] for i in range(nodes.rows_dev)]
            rows.append(pad)
        out[parcel.at[name], :] = jnp.concatenate(rows, axis=0)
    out[parcel.at["step"], :] = jnp.concatenate([mass_step[...], pad], axis=0)
    rows = []
    for t in range(parcel.tiles):
        rows += [x[t], u[t], v[t], k[t : t + 1, :], step[t : t + 1, :]]
    out[parcel.at["points"], :] = jnp.concatenate(rows, axis=0)
    for p in range(parcel.patches):
        first = parcel.at["matrix"].start + p * LANES
        out[first : first + LANES, :] = matrix[p]
    out[parcel.at["misc"], :] = jnp.full((parcel.at["misc"].stop - parcel.at["misc"].start, LANES), -1.0, f32)
    for name, ref in (
        ("nodes", ids), ("quad", quad), ("modulus", modulus), ("blend", blend), ("left", left), ("right", right),
    ):
        out[parcel.at[name], : ref.shape[1]] = ref[...].astype(f32)
    for p in range(2 * parcel.patches):
        row = parcel.at["tile"].start + p
        out[row : row + 1, :] = jnp.full((1, LANES), patch_tile[p], jnp.int32).astype(f32)
    out[parcel.at["elements"], :] = elements[...].astype(f32)
    out[parcel.at["grad"], : grad.shape[1]] = grad[...]


def start_kernel(
    nodes, parcel, own, partner, table, vel, step, pack, matrices, ids, shared, patch_rows, elements,
    grad, quad, modulus,
):
    rank = lax.axis_index("blk")
    half, tiles, patches = nodes.half, parcel.tiles, parcel.patches
    for order, (side, ref) in enumerate(((rank, own), (1 - rank, partner))):
        for name, out in (("disp", table), ("vel", vel)):
            for c in range(2):
                at = pl.multiple_of(c * nodes.rows + side * half, 8)
                first = parcel.at[name].start + c * half
                out[pl.ds(at, half), :] = ref[first : first + half, :]
        step[pl.ds(pl.multiple_of(side * half, 8), half), :] = ref[parcel.at["step"], :]
        for t in range(tiles):
            first = parcel.at["points"].start + 8 * t
            pack[side * tiles + t] = ref[first : first + 8, :]
        for p in range(patches):
            k = order * patches + p
            first = parcel.at["matrix"].start + p * LANES
            matrices[k] = ref[first : first + LANES, :]
            row = parcel.at["nodes"].start + p
            ids[:, k * LANES : (k + 1) * LANES] = ref[row : row + 1, :].astype(jnp.int32)
            for n, name in enumerate(("blend", "tile")):
                row = parcel.at[name].start + side * patches + p
                patch_rows[2 * patches * n + k : 2 * patches * n + k + 1, :] = own[pl.ds(row, 1), :]
    for n, name in enumerate(("left", "right")):
        shared[:, n * LANES : (n + 1) * LANES] = own[parcel.at[name], :].astype(jnp.int32)
    elements[...] = own[parcel.at["elements"], :].astype(jnp.int32)
    grad[...] = own[parcel.at["grad"], : grad.shape[1]]
    quad[...] = own[parcel.at["quad"], : quad.shape[1]]
    modulus[...] = own[parcel.at["modulus"], :]
    picked = nodes.pick(table[...], ids[...])
    blend_tiles(picked, patch_rows, matrices, pack)


GATHER_BLOCK = 16
ASSEMBLY_BLOCK = 32


def block_ids(ids, step, block):
    return jnp.concatenate([ids[pl.ds(step * block + k, 1), :] for k in range(block)], axis=1)


def stress_kernel(nodes, table, ids, modulus, quad, grad, force, cat, disp):
    local, elems = ids.shape
    n = nodes.rows // 2
    n2 = nodes.rows
    block = GATHER_BLOCK
    cat[...] = jnp.concatenate(split(nodes.wide_rows(table), 2), axis=0)

    def gather(step, carry):
        mask, onehot = nodes.wide_masks(block_ids(ids, step, block))
        both = dot(cat[...], onehot, NN)
        rows = both[:n2] + both[n2:]
        for c in range(2):
            got = jnp.sum(jnp.where(mask, rows[c * n : (c + 1) * n], 0.0), axis=0, keepdims=True)
            for k in range(block):
                disp[pl.ds(c * local + step * block + k, 1), :] = got[:, k * elems : (k + 1) * elems]
        return carry

    lax.fori_loop(0, local // block, gather, 0)
    g = grad[...]
    half = g.shape[0] // 2
    gx = dot(g, disp[:local], NN, HIGHEST)
    gy = dot(g, disp[local:], NN, HIGHEST)
    exx = gx[:half]
    eyy = gy[half:]
    exy = 0.5 * (gx[half:] + gy[:half])
    stiffen = 1.0 + exx * exx + eyy * eyy + 2.0 * exy * exy
    weights = jnp.broadcast_to(quad[...], (half, half))
    eye = lax.broadcasted_iota(jnp.int32, (half, half), 0) == lax.broadcasted_iota(
        jnp.int32, (half, half), 1
    )
    column = jnp.sum(jnp.where(eye, weights, 0.0), axis=1, keepdims=True)
    scaled = modulus[...] * column * stiffen
    trace = exx + eyy
    s_xx = scaled * (trace + 2.0 * exx)
    s_yy = scaled * (trace + 2.0 * eyy)
    s_xy = scaled * 2.0 * exy
    gt = g.T
    fx = dot(gt, jnp.concatenate([s_xx, s_xy], axis=0), NN, HIGHEST)
    fy = dot(gt, jnp.concatenate([s_xy, s_yy], axis=0), NN, HIGHEST)
    both = jnp.concatenate([fx, fy], axis=0)
    high = both.astype(bf16).astype(f32)
    force[0] = high
    force[1] = both - high


def assembly_kernel(nodes, ids, force, out, acc):
    local, _ = ids.shape
    n2 = nodes.rows
    block = ASSEMBLY_BLOCK
    acc[...] = jnp.zeros_like(acc)

    def scatter(step, carry):
        mask, onehot = nodes.wide_masks(block_ids(ids, step, block))
        placed = []
        for part in range(2):
            for c in range(2):
                rows = [
                    force[part, pl.ds(c * local + step * block + k, 1), :] for k in range(block)
                ]
                placed.append(jnp.where(mask, jnp.concatenate(rows, axis=1), 0.0))
        both = dot(jnp.concatenate(placed, axis=0).astype(bf16), onehot, NT)
        acc[...] += both[:n2] + both[n2:]
        return carry

    lax.fori_loop(0, local // block, scatter, 0)
    for k in range(2):
        out[pl.ds(k, nodes.rows, stride=2), :] = acc[:, k * LANES : (k + 1) * LANES]


def side_of(order):
    odd = lax.rem(lax.axis_index("dom"), 2)
    return 2 * (1 - odd) if order == 0 else 2 * odd


def gather_tiles(own, even, odd, ext):
    tiles = own.shape[0]
    for place, ref in ((side_of(0), even), (1, own), (side_of(1), odd)):
        for t in range(tiles):
            tile = ref[t]
            ext[place * tiles + t] = jnp.concatenate(
                [tile[0:2], tile[0:2] + tile[2:4], tile[4:8]], axis=0
            )


CHUNK = 64


def pair_terms(x0, x1, y0, y1, far):
    o0 = far[0:1] - x0
    o1 = far[1:2] - x1
    d0 = far[2:3] - y0
    d1 = far[3:4] - y1
    rest_sq = o0 * o0 + o1 * o1
    rest_core = rest_sq + core_sq
    rest_len = rest_core * lax.rsqrt(rest_core)
    length_sq = (d0 * d0 + d1 * d1) + core_sq
    length = length_sq * lax.rsqrt(length_sq)
    stretch = length - rest_len
    bell = jnp.exp(rest_sq * (-1.0 / horizon_sq))
    soft = 1.0 + stretch * stretch * (1.0 / stretch_scale**2)
    return d0, d1, rest_core, rest_len, length, stretch, bell, soft


def own_columns(own, ext, cols):
    tiles = own.shape[0]
    turned = jnp.concatenate([ext[tiles + t] for t in range(tiles)], axis=0).T
    for t in range(tiles):
        for q in range(4):
            at = 8 * t + q
            cols[4 * t + q] = jnp.broadcast_to(turned[:, at : at + 1], (LANES, LANES))


def each_live_tile(fam_own, fam_par, live, body):
    rank = lax.axis_index("blk")
    dev, slots = fam_own.shape
    for side, fam in ((rank, fam_own), (1 - rank, fam_par)):
        for index in range(dev):
            tile = side * dev + index
            pl.when(tile < live[0])(
                functools.partial(body, tile, [fam[index, s] for s in range(slots)])
            )


def dilatation_kernel(fam_own, fam_par, live, own, even, odd, out, ext, cols, sums):
    tiles = own.shape[0]
    gather_tiles(own, even, odd, ext)
    own_columns(own, ext, cols)

    def body(tile, names):
        fars = [ext[name] for name in names]

        def chunk(i, carry):
            at = pl.multiple_of(i * CHUNK, CHUNK)
            x0, x1, u0, u1 = [cols[4 * tile + q, pl.ds(at, CHUNK), :] for q in range(4)]
            vol = jnp.zeros((CHUNK, LANES), f32)
            dil = jnp.zeros((CHUNK, LANES), f32)
            for far in fars:
                _, _, rest_core, rest_len, _, stretch, bell, soft = pair_terms(x0, x1, u0, u1, far)
                influence = bell * pl.reciprocal(soft)
                vol = vol + influence * rest_core
                dil = dil + influence * rest_len * stretch
            sums[tile, 0, pl.ds(at, CHUNK), :] = vol
            sums[tile, 1, pl.ds(at, CHUNK), :] = dil
            return carry

        lax.fori_loop(0, LANES // CHUNK, chunk, 0)

    each_live_tile(fam_own, fam_par, live, body)
    total = dot(jnp.ones((8, LANES), f32), sums[...].reshape(2 * tiles * LANES, LANES), NT, HIGHEST)
    parts = [total[:1, n * LANES : (n + 1) * LANES] for n in range(2 * tiles)]
    volume = jnp.concatenate(parts[0::2], axis=0)
    theta = 2.0 * jnp.concatenate(parts[1::2], axis=0) / volume
    k = jnp.concatenate([own[t, 6:7, :] for t in range(tiles)], axis=0)
    scale = 4.0 * k / volume
    alpha = 2.0 * k * theta / volume - scale * (0.5 * theta)
    alive = lax.broadcasted_iota(jnp.int32, (tiles, LANES), 0) < live[0]
    out[:tiles, :] = jnp.where(alive, alpha, 0.0)
    out[tiles:, :] = jnp.where(alive, scale, 0.0)


def bond_kernel(fam_own, fam_par, live, own, even, odd, bonds, own_sums, ext, cols, sums):
    tiles = own.shape[0]
    gather_tiles(own, even, odd, ext)
    own_columns(own, ext, cols)

    def body(tile, names):
        fars = [ext[name] for name in names]

        def chunk(i, carry):
            at = pl.multiple_of(i * CHUNK, CHUNK)
            x0, x1, u0, u1 = [cols[4 * tile + q, pl.ds(at, CHUNK), :] for q in range(4)]
            acc = [jnp.zeros((CHUNK, LANES), f32)] * 4
            for s, far in enumerate(fars):
                d0, d1, _, rest_len, length, stretch, bell, soft = pair_terms(x0, x1, u0, u1, far)
                over = bell * pl.reciprocal(soft * length)
                by_rest = over * rest_len
                by_stretch = over * stretch
                terms = [by_rest * d0, by_rest * d1, by_stretch * d0, by_stretch * d1]
                for q, term in enumerate(terms):
                    bonds[tile, s, q, pl.ds(at, CHUNK), :] = term
                acc = [a + term for a, term in zip(acc, terms)]
            for q in range(4):
                sums[tile, q, pl.ds(at, CHUNK), :] = acc[q]
            return carry

        lax.fori_loop(0, LANES // CHUNK, chunk, 0)

    each_live_tile(fam_own, fam_par, live, body)
    total = dot(jnp.ones((8, LANES), f32), sums[...].reshape(4 * tiles * LANES, LANES), NT, HIGHEST)
    for t in range(tiles):
        for q in range(4):
            at = (4 * t + q) * LANES
            own_sums[t, q : q + 1, :] = total[:1, at : at + LANES]


def force_kernel(
    nodes, last, fam_own, fam_par, live, pack, ac, ac_even, ac_odd, bonds, own_sums,
    el_own, el_par, ids, matrices, patch_rows, shared, *refs,
):
    if last:
        nodal, for_even, for_odd, disp_out, vel_out, ext, sums, held = refs
    else:
        nodal, for_even, for_odd, state, ext, sums, held = refs
    rank = lax.axis_index("blk")
    tiles = pack.shape[0]
    dev, _ = fam_own.shape
    for place, ref in ((side_of(0), ac_even), (1, ac), (side_of(1), ac_odd)):
        for t in range(tiles):
            ext[place * tiles + t, 0:1, :] = ref[t : t + 1, :]
            ext[place * tiles + t, 1:2, :] = ref[tiles + t : tiles + t + 1, :]

    def body(tile, names):
        fars = [ext[name] for name in names]

        def chunk(i, carry):
            at = pl.multiple_of(i * CHUNK, CHUNK)
            f = [jnp.zeros((CHUNK, LANES), f32)] * 2
            for s, far in enumerate(fars):
                w = [bonds[tile, s, q, pl.ds(at, CHUNK), :] for q in range(4)]
                f = [f[c] + (w[c] * far[0:1] + w[2 + c] * far[1:2]) for c in range(2)]
            for c in range(2):
                sums[tile, c, pl.ds(at, CHUNK), :] = f[c]
            return carry

        lax.fori_loop(0, LANES // CHUNK, chunk, 0)

    each_live_tile(fam_own, fam_par, live, body)
    total = dot(jnp.ones((8, LANES), f32), sums[...].reshape(2 * tiles * LANES, LANES), NT, HIGHEST)
    for t in range(tiles):
        far_part = jnp.concatenate(
            [total[:1, (2 * t + c) * LANES : (2 * t + c + 1) * LANES] for c in range(2)], axis=0
        )
        near = own_sums[t]
        mine = ext[tiles + t]
        me = pack[t]
        force = (near[0:2] * mine[0:1] + near[2:4] * mine[1:2]) + far_part
        vel = me[4:6] + me[7:8] * force
        disp = me[2:4] + time_step * vel
        alive = lax.broadcasted_iota(jnp.int32, (6, LANES), 0) * 0 + t < live[0]
        held[t, 0:6, :] = jnp.where(alive, jnp.concatenate([force, disp, vel], axis=0), 0.0)

    if last:
        for t in range(dev):
            disp_out[t] = held[rank * dev + t, 2:4, :]
            vel_out[t] = held[rank * dev + t, 4:6, :]
    else:
        for t in range(tiles):
            mine = pack[t]
            now = held[t]
            state[t] = jnp.concatenate([mine[0:2], now[2:6], mine[6:8]], axis=0)
    patches = matrices.shape[0]
    reactions = []
    for k in range(patches):
        chosen = patch_rows[patches + k : patches + k + 1, :]
        force = jnp.zeros((2, LANES), f32)
        for t in range(tiles):
            force = force + jnp.where(chosen == float(t), held[t, 0:2, :], 0.0)
        weighted = force * patch_rows[k : k + 1, :]
        rows = jnp.concatenate([weighted, jnp.zeros((6, LANES), f32)], axis=0)
        reactions.append(dot(rows, matrices[k], NN, HIGHEST))
    react = jnp.concatenate(reactions, axis=1)
    total = nodes.spread([react[0:1], react[1:2]], ids[...]) - (el_own[...] + el_par[...])
    nodal[...] = total
    picked = nodes.pick(total, shared[...])
    low, high = [
        jnp.concatenate(
            [picked[0][:, at : at + LANES], picked[1][:, at : at + LANES], jnp.zeros((6, LANES), f32)],
            axis=0,
        )
        for at in (0, LANES)
    ]
    even_is_high = side_of(0) == 2
    for_even[...] = jnp.where(even_is_high, high, low)
    for_odd[...] = jnp.where(even_is_high, low, high)


def add_border(nodes, total, shared, even, odd):
    dom = lax.axis_index("dom")
    ends = lax.axis_size("dom") - 1
    even_is_high = side_of(0) == 2
    low = jnp.where(dom > 0, jnp.where(even_is_high, odd[...], even[...]), 0.0)
    high = jnp.where(dom < ends, jnp.where(even_is_high, even[...], odd[...]), 0.0)
    rows = jnp.concatenate([low, high], axis=1)
    return total + nodes.spread([rows[0:1], rows[1:2]], shared)


def update_kernel(
    nodes, nodal, table, vel, step, from_even, from_odd, shared, ids, matrices, patch_rows, state,
    table_out, vel_out, pack,
):
    force = add_border(nodes, nodal[...], shared[...], from_even, from_odd)
    steps = step[...]
    now = vel[...] + jnp.concatenate([steps, steps], axis=0) * force
    vel_out[...] = now
    disp = table[...] + time_step * now
    table_out[...] = disp
    pack[...] = state[...]
    picked = nodes.pick(disp, ids[...])
    blend_tiles(picked, patch_rows, matrices, pack)


def final_kernel(
    nodes, nodal, table, vel, step, from_even, from_odd, shared, disp_out, vel_out, f_s, v_s,
):
    rank = lax.axis_index("blk")
    force = add_border(nodes, nodal[...], shared[...], from_even, from_odd)
    steps = step[...]
    now = vel[...] + jnp.concatenate([steps, steps], axis=0) * force
    v_s[...] = now
    f_s[...] = table[...] + time_step * now
    for out, held in ((disp_out, f_s), (vel_out, v_s)):
        for c in range(2):
            at = pl.multiple_of(c * nodes.rows + rank * nodes.half, 8)
            rows = held[pl.ds(at, nodes.half), :]
            for i in range(nodes.rows_dev):
                out[c : c + 1, i * LANES : (i + 1) * LANES] = rows[i : i + 1]


def call(kernel, outs, scalars, arrays, scratch=(), flops=0, vmem=4, spec=VM):
    size = sum(a.size * 4 for a in arrays) + sum(o.size * 4 for o in outs)
    return pl.pallas_call(
        kernel,
        out_shape=list(outs),
        in_specs=[SM] * len(scalars) + [spec] * len(arrays),
        out_specs=[VM] * len(outs),
        scratch_shapes=list(scratch),
        cost_estimate=pl.CostEstimate(flops=flops, bytes_accessed=size, transcendentals=0),
        compiler_params=pltpu.CompilerParams(vmem_limit_bytes=int(vmem * 2**20)),
    )(*scalars, *arrays)


def shape(*dims, dtype=f32):
    return jax.ShapeDtypeStruct(dims, dtype)


def shards(
    pd_disp, pd_vel, pd_coord, pd_modulus, pd_step, family_tile_lists, live_tiles, patch_tile,
    patch_blend, patch_nodes, patch_matrix, fe_disp, fe_vel, fe_step, fe_modulus, element_nodes,
    shape_grad, quad_weight, shared_left, shared_right,
):
    doms = lax.axis_size("dom")
    dev = pd_disp.shape[0]
    tiles = 2 * dev
    patches = patch_matrix.shape[0]
    slots = family_tile_lists.shape[1]
    nodes = Nodes(fe_disp.shape[1])
    n2 = 2 * nodes.rows
    local, elems = element_nodes.shape

    def swap(x):
        return lax.ppermute(x, "blk", [(0, 1), (1, 0)])

    def place(dom, core):
        return 2 * dom + core

    even_pairs, odd_pairs = [], []
    for dom in range(doms):
        for core in range(2):
            other = dom - 1 if dom % 2 == 0 else dom + 1
            even_pairs.append((place(dom, core), place(dom ^ 1, core)))
            inside = 0 <= other < doms
            odd_pairs.append((place(dom, core), place(other, core) if inside else place(dom, 1 - core)))

    def exchange(for_even, for_odd):
        from_even = lax.ppermute(for_even, ("dom", "blk"), even_pairs)
        from_odd = lax.ppermute(for_odd, ("dom", "blk"), odd_pairs)
        return from_even, from_odd

    given = [
        patch_matrix, patch_nodes, fe_disp, pd_coord, pd_disp, pd_vel, pd_modulus, pd_step, fe_vel,
        fe_step.reshape(-1, LANES), shared_left, shared_right, element_nodes,
        shape_grad.reshape(-1, local), quad_weight[None, :], fe_modulus[None, :], patch_blend,
        patch_tile,
    ]
    spaces = [pltpu.VMEM] * (len(given) - 1) + [pltpu.SMEM]
    parcel = Parcel(nodes, dev, patches, local)
    (own,) = call(
        functools.partial(pack_kernel, nodes, parcel, len(given)),
        [shape(parcel.rows, LANES)],
        [], given,
        [space(x.shape, x.dtype) for space, x in zip(spaces, given)]
        + [pltpu.SemaphoreType.DMA((len(given),))],
        spec=HBM,
        vmem=63,
    )
    partner = swap(own)
    fam_par = swap(family_tile_lists)
    lists = [family_tile_lists, fam_par, live_tiles]
    int32 = jnp.int32
    table, vel, step, pack, matrices, ids, shared, patch_rows, elements, grad, quad, modulus = call(
        functools.partial(start_kernel, nodes, parcel),
        [
            shape(n2, LANES), shape(n2, LANES), shape(nodes.rows, LANES), shape(tiles, 8, LANES),
            shape(2 * patches, LANES, LANES), shape(1, 2 * patches * LANES, dtype=int32),
            shape(1, 2 * LANES, dtype=int32), shape(4 * patches, LANES),
            shape(local, elems, dtype=int32), shape(2 * local, local), shape(1, local), shape(1, elems),
        ],
        [],
        [own, partner],
    )
    for section in range(2):
        last = section == 1
        packs = [pack, *exchange(pack, pack)]
        (force_el,) = call(
            functools.partial(stress_kernel, nodes),
            [shape(2, 2 * local, elems)],
            [],
            [table, elements, modulus, quad, grad],
            [pltpu.VMEM((n2, 2 * LANES), bf16), pltpu.VMEM((2 * local, elems), f32)],
            flops=10**9, vmem=16,
        )
        (ac,) = call(
            dilatation_kernel,
            [shape(2 * tiles, LANES)],
            lists,
            packs,
            [
                pltpu.VMEM((3 * tiles, 8, LANES), f32),
                pltpu.VMEM((4 * tiles, LANES, LANES), f32),
                pltpu.VMEM((tiles, 2, LANES, LANES), f32),
            ],
        )
        acs = [ac, *exchange(ac, ac)]
        (el_own,) = call(
            functools.partial(assembly_kernel, nodes),
            [shape(n2, LANES)],
            [],
            [elements, force_el],
            [pltpu.VMEM((nodes.rows, 2 * LANES), f32)],
            flops=10**9, vmem=16,
        )
        el_par = swap(el_own)
        bonds, own_sums = call(
            bond_kernel,
            [shape(tiles, slots, 4, LANES, LANES), shape(tiles, 8, LANES)],
            lists,
            packs,
            [
                pltpu.VMEM((3 * tiles, 8, LANES), f32),
                pltpu.VMEM((4 * tiles, LANES, LANES), f32),
                pltpu.VMEM((tiles, 4, LANES, LANES), f32),
            ],
            vmem=8,
        )
        outs = [shape(n2, LANES), shape(8, LANES), shape(8, LANES)]
        if last:
            outs += [shape(dev, 2, LANES)] * 2
        else:
            outs += [shape(tiles, 8, LANES)]
        nodal, for_even, for_odd, *rest = call(
            functools.partial(force_kernel, nodes, last),
            outs,
            lists,
            [
                pack, *acs, bonds, own_sums, el_own, el_par, ids, matrices, patch_rows,
                shared,
            ],
            [
                pltpu.VMEM((3 * tiles, 8, LANES), f32),
                pltpu.VMEM((tiles, 2, LANES, LANES), f32),
                pltpu.VMEM((tiles, 8, LANES), f32),
            ],
            vmem=8,
        )
        from_even, from_odd = exchange(for_even, for_odd)
        if not last:
            table, vel, pack = call(
                functools.partial(update_kernel, nodes),
                [shape(n2, LANES), shape(n2, LANES), shape(tiles, 8, LANES)],
                [],
                [
                    nodal, table, vel, step, from_even, from_odd, shared, ids, matrices,
                    patch_rows, rest[0],
                ],
            )
        else:
            pd_disp, pd_vel = rest
            fe_disp, fe_vel = call(
                functools.partial(final_kernel, nodes),
                [shape(*fe_disp.shape)] * 2,
                [],
                [nodal, table, vel, step, from_even, from_odd, shared],
                [pltpu.VMEM((n2, LANES), f32)] * 2,
            )
    return (pd_disp, pd_vel, fe_disp, fe_vel)


def solution(mesh):
    return jax.shard_map(
        shards,
        mesh=mesh,
        in_specs=(
            P(("dom", "blk"), None, None),
            P(("dom", "blk"), None, None),
            P(("dom", "blk"), None, None),
            P(("dom", "blk"), None),
            P(("dom", "blk"), None),
            P(("dom", "blk"), None),
            P("dom"),
            P("dom"),
            P("dom", None),
            P(("dom", "blk"), None),
            P(("dom", "blk"), None, None),
            P(None, ("dom", "blk")),
            P(None, ("dom", "blk")),
            P(("dom", "blk")),
            P(("dom", "blk")),
            P(None, ("dom", "blk")),
            P(),
            P(),
            P("dom", None),
            P("dom", None),
        ),
        out_specs=(
            P(("dom", "blk"), None, None),
            P(("dom", "blk"), None, None),
            P(None, ("dom", "blk")),
            P(None, ("dom", "blk")),
        ),
        check_vma=False,
    )
```
